512 devices in a mesh: rep: 16 (over x_lo, y, core), ep: 32 (over z, x_hi).
Axes of the slice: x: 4 (x_hi: 2, x_lo: 2; x = x_hi * 2 + x_lo), y: 4, z: 16, core: 2. Of those that a mesh axis runs over, the one named last changes fastest.
Arguments:
- tokens: bfloat16 [65536, 3584], P(('rep', 'ep')), parts along dimension 0, may hold values from -6 to 6
- route_token: int32 [32768], P(('rep', 'ep')), parts along dimension 0, may hold values from 0 to 127
- route_expert: int32 [32768, 1], P(('rep', 'ep')), parts along dimension 0, may hold values from 0 to 3; in each aligned block of 64 rows (0 to 63, 64 to 127, ...) at most 24 rows name the same one
- route_gate: float32 [32768], P(('rep', 'ep')), parts along dimension 0, may hold values from 0.25 to 2.5
- w_in: bfloat16 [32, 3584, 256], P('ep'), may hold values from -0.09375 to 0.09375
- w_out: bfloat16 [32, 128, 3584], P('ep'), may hold values from -0.1875 to 0.1875
- swap_pairs: int32 [16], replicated, may hold values 0 or 1
Outputs:
- mixed: bfloat16 [65536, 3584], P(('rep', 'ep')), parts along dimension 0
- saved_hidden: bfloat16 [512, 768, 128], P(('rep', 'ep')), parts along dimension 0
The draws below stay inside these ranges and needn't reach their ends.
There are 16 independent parts, one for each index of `rep`. The reference program is written for one: setup_inputs(seed, part) draws one part's arguments, and reference() takes and returns one part's arrays. A program takes and returns all parts, laid end to end along the dimension named above; an argument that names none is the same for every part. Nothing has to cross between parts.
Inputs may be any that keep to these rules, and one draw needn't show every extreme that they name: `route_expert`: in each block of 64 rows (the rows of one device) no expert is named by more than 24 rows, and some block names an expert exactly 24 times.
All inputs are finite; a program needn't handle non-finite values.
Results may differ from the reference program's by a relative error of at most 0.0057.
Values may be sent and summed in bfloat16 or wider, within the bound.
A program may use at most 64 MiB of HBM per device.

```python
import math
import jax
import jax.numpy as jnp
import numpy as np
from jax import lax

D = 3584
HS = 128
SLICES = 8
TOK_DEV = 128
R_DEV = 64
HIDDEN_SIZE = 1024
EXPERTS = 4
C = 24
TOKENS = 4096
ROWS = 2048
N_EP = 32


def place_ends(entries, key, smallest, top_value):
    longest = entries.shape.index(max(entries.shape))
    spots = []
    for shift in (0, 1):
        where = [jax.random.randint(jax.random.fold_in(key, axis), (), 0, length) for axis, length in enumerate(entries.shape)]
        where[longest] = (where[longest] + shift) % entries.shape[longest]
        spots.append(tuple(where))
    return entries.at[spots[0]].set(smallest).at[spots[1]].set(top_value)


def levels(own_key, extent, shards, least, high):
    factor_of = 1.0
    for axis_at, parts in shards:
        steps = jax.random.uniform(jax.random.fold_in(jax.random.fold_in(own_key, 6), axis_at), (parts,), jnp.float32, least / len(shards), high / len(shards))
        factor_of = factor_of * jnp.repeat(jnp.exp(steps), extent[axis_at] // parts).reshape((-1,) + (1,) * (len(extent) - 1 - axis_at))
    return factor_of


def deal_out(stream_key, own, number, rows, number_of, top, reach, slope):
    order = jax.random.permutation(stream_key, number_of)
    packed, common = portions_of(number_of, rows * top, reach, slope, True), portions_of(number_of, rows * top, reach, slope, False)
    places = jnp.arange(number_of)

    def named(tallies, turn):
        used = int((tallies > 0).sum())
        fixed = max(1, used // 4)
        passed = fixed + (places - fixed + turn * (used - fixed)) % max(1, number_of - fixed)
        return jnp.zeros((number_of,), jnp.int32).at[order[jnp.where(places < fixed, places, passed)]].set(jnp.asarray(tallies, jnp.int32))

    tallies = jnp.where(number % 4 == 0, named(packed, number // 4), named(common, number - number // 4 - 1))
    mixed = jax.random.permutation(jax.random.fold_in(own, 3), number_of)
    donor, taker = mixed[0:number_of // 2 * 2:2], mixed[1:number_of // 2 * 2:2]
    slack = jnp.minimum(tallies[donor] - 1, reach - tallies[taker]) // 2
    slack = jnp.where((donor == order[0]) | (taker == order[0]) | (tallies[taker] == 0), 0, jnp.maximum(slack, 0))
    passed = jax.random.randint(jax.random.fold_in(own, 4), (number_of // 2,), 0, 1 << 20) % (slack + 1)
    tallies = tallies.at[donor].add(-passed).at[taker].add(passed)
    items = jnp.searchsorted(jnp.cumsum(tallies), jnp.arange(rows * top), side="right").astype(jnp.int32)
    table = items.reshape(top, rows).T
    table = table[jax.random.permutation(jax.random.fold_in(own, 1), rows)]
    turn = jax.random.randint(jax.random.fold_in(own, 2), (rows, 1), 0, top)
    return jnp.take_along_axis(table, (jnp.arange(top)[None, :] + turn) % top, axis=1)


def portions_of(count, total, reach, lean, full):
    weights = [(1 << 20) // math.isqrt(grade ** lean) + 1 for grade in range(1, count + 1)]
    largest = reach if full else min(reach, max(-(-total // count), total * weights[0] // sum(weights)))
    least = 1 if total - largest >= count - 1 else 0
    holding, surplus = [largest] + [least] * (count - 1), total - largest - least * (count - 1)
    while surplus > 0:
        candidates = [i for i in range(1, count) if holding[i] < largest] or [i for i in range(1, count) if holding[i] < reach]
        pool, left = sum([weights[i] for i in candidates]), surplus
        for i in candidates:
            addition = min(reach - holding[i], max(1, left * weights[i] // pool), surplus)
            holding[i] = holding[i] + addition
            surplus = surplus - addition
    return np.array(holding)


def bell_draw(own_key, dims, width, bound, cuts=(), held_as=jnp.bfloat16):
    drawn = width * jax.random.normal(own_key, dims, jnp.float32)
    if cuts:
        drawn = drawn * levels(own_key, dims, cuts, -0.22, 0.18)
    return jnp.clip(drawn, -bound, bound).astype(held_as)


def setup_inputs(seed: int = 0, part: int = 0) -> dict:
    splits = jax.random.split(jax.random.key(seed), 8)
    part_splits = jax.random.split(jax.random.fold_in(splits[7], part), 8)
    tokens = bell_draw(part_splits[0], (TOKENS, D), 1.0, 6.0, ((0, 32),))
    route_token = place_ends(jax.random.randint(part_splits[1], (ROWS,), 0, TOK_DEV), jax.random.fold_in(part_splits[1], 1), 0, TOK_DEV - 1).astype(jnp.int32)
    route_expert_keys = jax.random.split(jax.random.fold_in(part_splits[2], 1), ROWS // R_DEV)
    route_expert_turns = jax.random.permutation(jax.random.fold_in(part_splits[2], 3), ROWS // R_DEV)
    route_expert = jax.vmap(lambda own, number: deal_out(jax.random.fold_in(part_splits[2], 2), own, number, R_DEV, EXPERTS, 1, C, 1))(route_expert_keys, route_expert_turns).reshape((ROWS, 1))
    route_gate = jnp.clip(0.25 + 2.25 * jax.random.uniform(part_splits[3], (ROWS,), jnp.float32) ** levels(part_splits[3], (ROWS,), ((0, 32),), -0.2, 0.2), 0.25, 2.5)
    w_in = bell_draw(splits[4], (N_EP, D, 2 * HS), D ** -0.5, 0.09375, ((0, 32),))
    w_out = bell_draw(splits[5], (N_EP, HS, D), HIDDEN_SIZE ** -0.5, 0.1875, ((0, 32),))
    swap_pairs = place_ends((jax.random.randint(splits[6], (N_EP // 2,), 0, 2) < 1).astype(jnp.int32), jax.random.fold_in(splits[6], 1), 0, 1)
    return dict(tokens=tokens, route_token=route_token, route_expert=route_expert, route_gate=route_gate, w_in=w_in, w_out=w_out, swap_pairs=swap_pairs)


def pick_rows(local_block, index_block):
    return local_block[index_block]


def reference(tokens, route_token, route_expert, route_gate, w_in, w_out, swap_pairs):
    expert_ids = route_expert[:, 0].reshape(N_EP, R_DEV)
    token_ids = route_token.reshape(N_EP, R_DEV)
    expert_range = jnp.arange(EXPERTS, dtype=jnp.int32)
    slot_range = jnp.arange(C, dtype=jnp.int32)
    expert_hits = (expert_ids[:, :, None] == expert_range[None, None, :]).astype(jnp.int32)
    slot_index = jnp.sum((jnp.cumsum(expert_hits, axis=1) - 1) * expert_hits, axis=2)
    slot_table = ((expert_ids[:, None, None, :] == expert_range[None, :, None, None])
                  & (slot_index[:, None, None, :] == slot_range[None, None, :, None])).astype(jnp.float32)
    local_tokens = tokens.reshape(N_EP, TOK_DEV, D)
    picked = jax.vmap(pick_rows)(local_tokens, token_ids).astype(jnp.float32)
    expert_buf = jnp.einsum("qecr,qrd->eqcd", slot_table, picked, precision=lax.Precision.HIGHEST)
    expert_buf = expert_buf.astype(jnp.bfloat16).reshape(EXPERTS, N_EP * C, D)

    def block_step(totals, block_index):
        expert_index = block_index // SLICES
        inputs = lax.dynamic_index_in_dim(expert_buf, expert_index, 0, keepdims=False)
        weight_in = lax.dynamic_index_in_dim(w_in, block_index, 0, keepdims=False)
        weight_out = lax.dynamic_index_in_dim(w_out, block_index, 0, keepdims=False)
        gate_up = jnp.dot(inputs, weight_in, preferred_element_type=jnp.float32)
        hidden = (jax.nn.silu(gate_up[:, :HS]) * gate_up[:, HS:]).astype(jnp.bfloat16)
        partial_value = jnp.dot(hidden, weight_out, preferred_element_type=jnp.float32).astype(jnp.bfloat16)
        totals = totals.at[expert_index].add(partial_value.astype(jnp.float32))
        return totals, hidden

    start = jnp.zeros((EXPERTS, N_EP * C, D), jnp.float32)
    combined, hiddens = lax.scan(block_step, start, jnp.arange(N_EP, dtype=jnp.int32))
    flat_out = combined.reshape(EXPERTS * N_EP * C, D)
    device_ids = jnp.arange(N_EP, dtype=jnp.int32)
    flat_index = (expert_ids * (N_EP * C) + device_ids[:, None] * C + slot_index).reshape(-1)
    row_values = flat_out[flat_index]
    weighted = route_gate[:, None] * row_values
    token_index = (device_ids[:, None] * TOK_DEV + token_ids).reshape(-1)
    mixed = jax.ops.segment_sum(weighted, token_index, num_segments=TOKENS).astype(jnp.bfloat16)
    half_axis = N_EP // 2
    pair_flag = swap_pairs[device_ids % half_axis]
    served_block = jnp.where(pair_flag == 1, (device_ids + half_axis) % N_EP, device_ids)
    saved_hidden = hiddens[served_block]
    return mixed, saved_hidden
```

```python
import functools

import jax
import jax.numpy as jnp
from jax import lax
from jax.experimental import pallas as pl
from jax.experimental.pallas import tpu as pltpu
from jax.sharding import PartitionSpec as P

MESH = pl.DeviceIdType.MESH
BF = jnp.bfloat16
F32 = jnp.float32
CAP = 24
D = 3584
HS = 128
NO = 16
NI = 32
KI = D // NI
DH = D // 2


def loop(n, body):
    def step(i, carry):
        body(i)
        return carry

    lax.fori_loop(0, n, step, 0)


def kernel(
    tokens, tok_row, exp_row, exp_col, gate_row, swap, w_in, w_out,
    mixed, saved,
    xs, rx, pb, hs, out, ha, hb, wi, wo, gmat,
    r_send, r_recv, p_send, p_recv, h_send, ha_recv, hb_recv,
    wo_send, wo_recv, wi_send, wi_recv, co_send, co_recv, ci_send, ci_recv, loc,
):
    rep = lax.axis_index("rep")
    ep = lax.axis_index("ep")
    c = lax.rem(rep, 2)
    y = lax.rem(rep // 2, 4)
    xl = rep // 8
    xh = lax.rem(ep, 2)
    z = ep // 2
    x = 2 * xh + xl

    def dev(dx, dy, dz, dc):
        return ((lax.rem(dx, 2) * 4 + dy) * 2 + dc, dz * 2 + dx // 2)

    def plane(i):
        return lax.rem(x + i // 4, 4), lax.rem(y + lax.rem(i, 4), 4)

    ahead = lax.rem(z + 1 - 2 * c + 16, 16)
    behind = lax.rem(z - 1 + 2 * c + 16, 16)
    source = 4 * y + 2 * xl + c
    away = lax.rem((z - source) * (1 - 2 * c) + 32, 16)
    nxt = dev(x, y, ahead, c)
    mate = dev(x, y, z, 1 - c)

    barrier = pltpu.get_barrier_semaphore()

    def greet(target):
        pl.semaphore_signal(barrier, inc=1, device_id=target, device_id_type=MESH)

    def greet_plane(i):
        px, py = plane(i + 1)
        greet(dev(px, py, z, c))

    loop(15, greet_plane)
    greet(dev(x, y, behind, c))
    greet(mate)
    unit = lax.rem(z, 4)

    def greet_column(i):
        half = i // 16
        dz = lax.rem(i, 16)
        dx = 2 * xh + unit // 2
        dy = lax.rem(z + 8 * half, 16) // 4
        same = (dx == x) & (dy == y) & (dz == z)

        @pl.when(jnp.logical_not(same))
        def _():
            greet(dev(dx, dy, dz, c))

    loop(32, greet_column)
    own_a = ((unit // 2 == xl) & (z // 4 == y)).astype(jnp.int32)
    own_b = ((unit // 2 == xl) & (lax.rem(z + 8, 16) // 4 == y)).astype(jnp.int32)

    rows = exp_row.shape[1]
    earlier = (exp_col[...] == exp_row[...]) & (
        lax.broadcasted_iota(jnp.int32, (rows, rows), 0)
        < lax.broadcasted_iota(jnp.int32, (rows, rows), 1)
    )
    slot = jnp.sum(earlier.astype(F32), axis=0, keepdims=True).astype(jnp.int32)
    key = exp_row[...] * CAP + slot
    tok_hot = (lax.broadcasted_iota(jnp.int32, (128, rows), 0) == tok_row[...]).astype(F32)
    contract = (((1,), (1,)), ((), ()))
    place_all = (lax.broadcasted_iota(jnp.int32, (4 * CAP, rows), 0) == key).astype(F32)
    gmat[...] = lax.dot_general(
        tok_hot * gate_row[...], place_all, contract,
        precision=lax.Precision.HIGHEST, preferred_element_type=F32,
    )
    for e in range(4):
        place = (lax.broadcasted_iota(jnp.int32, (CAP, rows), 0) + CAP * e == key).astype(BF)
        pick = lax.dot_general(place, tok_hot.astype(BF), contract, preferred_element_type=F32).astype(BF)
        for n in range(7):
            cols = pl.ds(n * 512, 512)
            xs[e, :, cols] = jnp.dot(pick, tokens[:, cols], preferred_element_type=F32).astype(BF)

    pl.semaphore_wait(barrier, 49 - own_a - own_b)

    def wo_at(core, i):
        return wo.at[pl.ds(pl.multiple_of(128 * core + 16 * (i // 2), 16), 16), pl.ds(pl.multiple_of(DH * lax.rem(i, 2), 128), DH)]

    def wi_at(core, i):
        return wi.at[core, pl.ds(pl.multiple_of(KI * i, KI), KI)]

    def wo_src(i):
        return w_out.at[pl.ds(pl.multiple_of(16 * (i // 2), 16), 16), pl.ds(pl.multiple_of(DH * lax.rem(i, 2), 128), DH)]

    def wi_src(i):
        return w_in.at[pl.ds(pl.multiple_of(KI * i, KI), KI)]

    def remote(src, dst, send, recv, target):
        return pltpu.make_async_remote_copy(
            src_ref=src, dst_ref=dst, send_sem=send, recv_sem=recv,
            device_id=target, device_id_type=MESH,
        )

    keep_o = pltpu.make_async_copy(w_out, wo.at[pl.ds(pl.multiple_of(128 * c, 128), 128)], loc.at[0])
    keep_i = pltpu.make_async_copy(w_in, wi.at[c], loc.at[1])

    def chain_o(i, src):
        return remote(src, wo_at(c, i), wo_send.at[i], wo_recv.at[i], nxt)

    def chain_i(i, src):
        return remote(src, wi_at(c, i), wi_send.at[i], wi_recv.at[i], nxt)

    def mate_o(i, src, core):
        return remote(src, wo_at(core, i), co_send.at[i], co_recv.at[i], mate)

    def mate_i(i, src, core):
        return remote(src, wi_at(core, i), ci_send.at[i], ci_recv.at[i], mate)

    @pl.when(away == 0)
    def _():
        keep_o.start()
        keep_i.start()

        def first_o(i):
            chain_o(i, wo_src(i)).start()
            mate_o(i, wo_src(i), c).start()

        def first_i(i):
            chain_i(i, wi_src(i)).start()
            mate_i(i, wi_src(i), c).start()

        loop(NO, first_o)
        loop(NI, first_i)

    def row_copy(i):
        px, py = plane(i + 1)
        return remote(xs.at[py], rx.at[x, y], r_send.at[i], r_recv.at[i], dev(px, py, z, c))

    loop(15, lambda i: row_copy(i).start())
    mine = pltpu.make_async_copy(xs.at[y], rx.at[x, y], loc.at[2])
    mine.start()

    @pl.when(away > 0)
    def _():
        def relay_o(i):
            chain_o(i, wo_at(c, i)).wait_recv()

            @pl.when(away < 15)
            def _():
                chain_o(i, wo_at(c, i)).start()

            mate_o(i, wo_at(c, i), c).start()

        def relay_i(i):
            chain_i(i, wi_at(c, i)).wait_recv()

            @pl.when(away < 15)
            def _():
                chain_i(i, wi_at(c, i)).start()

            mate_i(i, wi_at(c, i), c).start()

        loop(NO, relay_o)
        loop(NI, relay_i)

    @pl.when(away == 0)
    def _():
        keep_o.wait()
        keep_i.wait()

    loop(NO, lambda i: mate_o(i, wo_at(1 - c, i), 1 - c).wait_recv())
    loop(NI, lambda i: mate_i(i, wi_at(1 - c, i), 1 - c).wait_recv())
    mine.wait()

    def row_arrival(i):
        px, py = lax.rem(x + 4 - (i + 1) // 4, 4), lax.rem(y + 4 - lax.rem(i + 1, 4), 4)
        remote(xs.at[py], rx.at[px, py], r_send.at[i], r_recv.at[i], dev(px, py, z, c)).wait_recv()

    loop(15, row_arrival)

    def part_copy(i):
        px, py = plane(i)
        return remote(pb.at[px, py], out.at[x, y], p_send.at[i], p_recv.at[i], dev(px, py, z, c))

    def hidden_copy(g, i):
        sx = lax.rem(x + g, 4)
        sy = i // 4
        s = lax.rem(i // 2, 2)
        half = lax.rem(i, 2)
        dz = lax.rem(4 * y + 2 * xl + s + 8 * half, 16)
        dx = 2 * xh + lax.rem(sx, 2)
        q = z * 2 + sx // 2
        same = (dx == x) & (sy == y) & (dz == z)
        src = hs.at[sx, sy, :, pl.ds(pl.multiple_of(HS * s, HS), HS)]
        return same, half, q, src, dev(dx, sy, dz, c)

    def send_hidden(g, i):
        same, half, q, src, target = hidden_copy(g, i)
        for k, (dst, recv) in enumerate(((ha, ha_recv), (hb, hb_recv))):
            @pl.when((half == k) & same)
            def _():
                pltpu.make_async_copy(src, dst.at[q], recv.at[q]).start()

            @pl.when((half == k) & jnp.logical_not(same))
            def _():
                remote(src, dst.at[q], h_send.at[g, i], recv.at[q], target).start()

    def sent_hidden(g, i):
        same, half, q, src, target = hidden_copy(g, i)

        @pl.when(jnp.logical_not(same))
        def _():
            remote(src, ha.at[q], h_send.at[g, i], ha_recv.at[q], target).wait_send()

    def group(step):
        g = lax.rem(step + 1, 4)
        sx = lax.rem(x + g, 4)
        block = rx[sx].reshape(4 * CAP, D)
        parts = []
        for s in range(2):
            gate_up = jnp.dot(block, wi[s], preferred_element_type=F32)
            v, u = gate_up[:, :HS], gate_up[:, HS:]
            parts.append((v / (1.0 + jnp.exp(-v)) * u).astype(BF))
        hidden = jnp.concatenate(parts, axis=1)
        hs[sx] = hidden.reshape(4, CAP, 2 * HS)
        for n in range(7):
            cols = pl.ds(n * 512, 512)
            partial = jnp.dot(hidden, wo[:, cols], preferred_element_type=F32).astype(BF)
            pb[sx, :, :, cols] = partial.reshape(4, CAP, 512)

        def leave(k):
            i = 4 * g + k

            @pl.when(i > 0)
            def _():
                part_copy(i).start()

        loop(4, leave)
        loop(16, lambda i: send_hidden(g, i))

    loop(4, group)
    own = pltpu.make_async_copy(pb.at[x, y], out.at[x, y], loc.at[3])
    own.start()

    def hidden_arrival(q):
        pltpu.make_async_copy(ha.at[q], ha.at[q], ha_recv.at[q]).wait()
        pltpu.make_async_copy(hb.at[q], hb.at[q], hb_recv.at[q]).wait()

    loop(32, hidden_arrival)
    flag = swap[lax.rem(ep, 16)]
    saved[...] = jnp.where(flag == 1, hb[...], ha[...])

    own.wait()

    def part_arrival(i):
        k = i + 1
        px, py = lax.rem(x + 4 - k // 4, 4), lax.rem(y + 4 - lax.rem(k, 4), 4)
        remote(pb.at[px, py], out.at[px, py], p_send.at[k], p_recv.at[k], dev(px, py, z, c)).wait_recv()

    loop(15, part_arrival)
    for n in range(7):
        cols = pl.ds(n * 512, 512)
        total = out[0, :, :, cols].astype(F32)
        for k in range(1, 4):
            total = total + out[k, :, :, cols].astype(F32)
        mixed[:, cols] = jnp.dot(
            gmat[...], total.reshape(4 * CAP, 512),
            precision=lax.Precision.HIGHEST, preferred_element_type=F32,
        ).astype(BF)

    loop(15, lambda i: row_copy(i).wait_send())
    loop(15, lambda i: part_copy(i + 1).wait_send())
    loop(64, lambda i: sent_hidden(i // 16, lax.rem(i, 16)))

    @pl.when(away < 15)
    def _():
        loop(NO, lambda i: chain_o(i, wo_at(c, i)).wait_send())
        loop(NI, lambda i: chain_i(i, wi_at(c, i)).wait_send())

    loop(NO, lambda i: mate_o(i, wo_at(c, i), c).wait_send())
    loop(NI, lambda i: mate_i(i, wi_at(c, i), c).wait_send())


def shards(tokens, route_token, route_expert, route_gate, w_in, w_out, swap_pairs):
    rows = route_token.shape[0]
    vmem = pl.BlockSpec(memory_space=pltpu.VMEM)
    hbm = pl.BlockSpec(memory_space=pl.ANY)
    dma = pltpu.SemaphoreType.DMA
    mixed, saved = pl.pallas_call(
        kernel,
        out_shape=(
            jax.ShapeDtypeStruct((128, D), BF),
            jax.ShapeDtypeStruct((32, CAP, HS), BF),
        ),
        in_specs=[vmem, vmem, vmem, vmem, vmem, pl.BlockSpec(memory_space=pltpu.SMEM), hbm, hbm],
        out_specs=(vmem, vmem),
        scratch_shapes=[
            pltpu.VMEM((4, CAP, D), BF),
            pltpu.VMEM((4, 4, CAP, D), BF),
            pltpu.VMEM((4, 4, CAP, D), BF),
            pltpu.VMEM((4, 4, CAP, 2 * HS), BF),
            pltpu.VMEM((4, 4, CAP, D), BF),
            pltpu.VMEM((32, CAP, HS), BF),
            pltpu.VMEM((32, CAP, HS), BF),
            pltpu.VMEM((2, D, 2 * HS), BF),
            pltpu.VMEM((2 * HS, D), BF),
            pltpu.VMEM((128, 4 * CAP), F32),
            dma((15,)), dma((15,)), dma((16,)), dma((16,)), dma((4, 16)), dma((32,)), dma((32,)),
            dma((NO,)), dma((NO,)), dma((NI,)), dma((NI,)), dma((NO,)), dma((NO,)), dma((NI,)), dma((NI,)),
            dma((4,)),
        ],
        compiler_params=pltpu.CompilerParams(
            collective_id=0, has_side_effects=True, vmem_limit_bytes=60 * 1024 * 1024
        ),
    )(
        tokens,
        route_token.reshape(1, rows),
        route_expert.reshape(1, rows),
        route_expert,
        route_gate.reshape(1, rows),
        swap_pairs,
        w_in[0],
        w_out[0],
    )
    return mixed, saved.reshape(1, 32 * CAP, HS)


def solution(mesh):
    return jax.shard_map(
        shards,
        mesh=mesh,
        in_specs=(
            P(("rep", "ep"), None),
            P(("rep", "ep")),
            P(("rep", "ep"), None),
            P(("rep", "ep")),
            P("ep", None, None),
            P("ep", None, None),
            P(),
        ),
        out_specs=(P(("rep", "ep"), None), P(("rep", "ep"), None, None)),
        check_vma=False,
    )
```

```python
import functools

import jax
import jax.numpy as jnp
from jax import lax
from jax.experimental import pallas as pl
from jax.experimental.pallas import tpu as pltpu
from jax.sharding import PartitionSpec as P

MESH = pl.DeviceIdType.MESH
BF = jnp.bfloat16
F32 = jnp.float32
CAP = 24
D = 3584
HS = 128
DH = D // 2
NI = 14
NO = 7
NC = NI + NO
LAG = 2


def loop(n, body):
    def step(i, carry):
        body(i)
        return carry

    lax.fori_loop(0, n, step, 0)


def kernel(
    tokens, tok_row, exp_row, exp_col, gate_row, swap, w_in, w_out,
    mixed, saved,
    xs, rx, pb, hs, out, ha, hb, wt, tr, gmat,
    ry_send, ry_recv, rx_send, rx_recv, p_send, p_recv, h_send, ha_recv, hb_recv,
    m_up, m_down, m_recv, o_up, o_down, o_recv, y_send, y_recv, c_send, c_recv, seed, loc,
):
    rep = lax.axis_index("rep")
    ep = lax.axis_index("ep")
    c = lax.rem(rep, 2)
    y = lax.rem(rep // 2, 4)
    xl = rep // 8
    xh = lax.rem(ep, 2)
    z = ep // 2
    x = 2 * xh + xl

    def dev(dx, dy, dz, dc):
        return ((lax.rem(dx, 2) * 4 + dy) * 2 + dc, dz * 2 + dx // 2)

    def plane(i):
        return lax.rem(x + i // 4, 4), lax.rem(y + lax.rem(i, 4), 4)

    def swapped(v):
        return v // 2 + 2 * lax.rem(v, 2)

    expert = swapped(y)
    half = lax.rem(y, 2)
    mate = dev(x, y, z, 1 - c)
    pair = dev(x, y + 1 - 2 * half, z, c)
    above = dev(x, y, lax.rem(z + 1, 16), c)
    below = dev(x, y, lax.rem(z + 15, 16), c)
    m_at = lax.rem(z - (4 * expert + 2 * xl + c) + 32, 16)
    o_at = lax.rem(m_at + 8, 16)

    barrier = pltpu.get_barrier_semaphore()

    def greet(target):
        pl.semaphore_signal(barrier, inc=1, device_id=target, device_id_type=MESH)

    def greet_plane(i):
        px, py = plane(i + 1)
        greet(dev(px, py, z, c))

    loop(15, greet_plane)
    greet(above)
    greet(below)
    greet(mate)
    unit = lax.rem(z, 4)

    def greet_column(i):
        turn = i // 16
        dz = lax.rem(i, 16)
        dx = 2 * xh + unit // 2
        dy = swapped(lax.rem(z + 8 * turn, 16) // 4)
        same = (dx == x) & (dy == y) & (dz == z)

        @pl.when(jnp.logical_not(same))
        def _():
            greet(dev(dx, dy, dz, c))

    loop(32, greet_column)
    own_a = ((unit // 2 == xl) & (swapped(z // 4) == y)).astype(jnp.int32)
    own_b = ((unit // 2 == xl) & (swapped(lax.rem(z + 8, 16) // 4) == y)).astype(jnp.int32)

    rows = exp_row.shape[1]
    earlier = (exp_col[...] == exp_row[...]) & (
        lax.broadcasted_iota(jnp.int32, (rows, rows), 0)
        < lax.broadcasted_iota(jnp.int32, (rows, rows), 1)
    )
    slot = jnp.sum(earlier.astype(F32), axis=0, keepdims=True).astype(jnp.int32)
    line = lax.shift_right_logical(exp_row[...], 1) + 2 * (exp_row[...] & 1)
    key = line * CAP + slot
    tok_hot = (lax.broadcasted_iota(jnp.int32, (128, rows), 0) == tok_row[...]).astype(F32)
    contract = (((1,), (1,)), ((), ()))
    place_all = (lax.broadcasted_iota(jnp.int32, (4 * CAP, rows), 0) == key).astype(F32)
    gmat[...] = lax.dot_general(
        tok_hot * gate_row[...], place_all, contract,
        precision=lax.Precision.HIGHEST, preferred_element_type=F32,
    )
    for e in range(4):
        place = (lax.broadcasted_iota(jnp.int32, (CAP, rows), 0) + CAP * e == key).astype(BF)
        pick = lax.dot_general(place, tok_hot.astype(BF), contract, preferred_element_type=F32).astype(BF)
        for n in range(7):
            cols = pl.ds(n * 512, 512)
            xs[e, :, cols] = jnp.dot(pick, tokens[:, cols], preferred_element_type=F32).astype(BF)

    pl.semaphore_wait(barrier, 50 - own_a - own_b)

    def remote(src, dst, send, recv, target):
        return pltpu.make_async_remote_copy(
            src_ref=src, dst_ref=dst, send_sem=send, recv_sem=recv,
            device_id=target, device_id_type=MESH,
        )

    def y_copy(k):
        py = lax.rem(y + k + 1, 4)
        return remote(xs.at[py], rx.at[x, y], ry_send.at[k], ry_recv.at[k], dev(x, py, z, c))

    def x_copy(k, n):
        sy = lax.rem(y + 4 - k, 4)
        return remote(
            rx.at[x, sy], rx.at[x, sy], rx_send.at[k, n], rx_recv.at[k, n],
            dev(lax.rem(x + n + 1, 4), y, z, c),
        )

    def x_arrival(k, n):
        sx, sy = lax.rem(x + 3 - n, 4), lax.rem(y + 4 - k, 4)
        remote(rx.at[sx, sy], rx.at[sx, sy], rx_send.at[k, n], rx_recv.at[k, n], pair).wait_recv()

    loop(3, lambda k: y_copy(k).start())
    mine = pltpu.make_async_copy(xs.at[y], rx.at[x, y], loc.at[2])
    mine.start()

    def seed_copy(i, dst, start):
        go = lambda d: d.start() if start else d.wait()

        @pl.when(i < NI)
        def _():
            rows_at = pl.ds(pl.multiple_of(DH * half + 128 * i, 128), 128)
            go(pltpu.make_async_copy(w_in.at[rows_at], dst.at[i], seed.at[i]))

        @pl.when(i >= NI)
        def _():
            cols_at = pl.ds(pl.multiple_of(256 * (2 * (i - NI) + half), 256), 256)
            go(pltpu.make_async_copy(w_out.at[:, cols_at], dst.at[i], seed.at[i]))

    own_half = wt.at[c, half]

    @pl.when(m_at == 0)
    def _():
        loop(NC, lambda i: seed_copy(i, own_half, True))
        loop(NC, lambda i: seed_copy(i, own_half, False))

    @pl.when(o_at == 0)
    def _():
        loop(NC, lambda i: seed_copy(i, tr, True))
        loop(NC, lambda i: seed_copy(i, tr, False))

    def stream(buf, at, up, down, recv):
        far = jnp.where(at > 8, 16 - at, at)
        goes_up = at <= 7
        goes_down = (at == 0) | (at >= 10)

        def to_above(i):
            return remote(buf.at[i], buf.at[i], up.at[i], recv.at[i], above)

        def to_below(i):
            return remote(buf.at[i], buf.at[i], down.at[i], recv.at[i], below)

        def pass_on(i):
            @pl.when(at != 0)
            def _():
                to_above(i).wait_recv()

            @pl.when(goes_up)
            def _():
                to_above(i).start()

            @pl.when(goes_down)
            def _():
                to_below(i).start()

        def settle():
            @pl.when(goes_up)
            def _():
                loop(NC, lambda i: to_above(i).wait_send())

            @pl.when(goes_down)
            def _():
                loop(NC, lambda i: to_below(i).wait_send())

        return far, pass_on, settle

    m_far, m_pass, m_settle = stream(own_half, m_at, m_up, m_down, m_recv)
    o_far, o_pass, o_settle = stream(tr, o_at, o_up, o_down, o_recv)

    def pair_copy(i):
        return remote(tr.at[i], wt.at[c, half, i], y_send.at[i], y_recv.at[i], pair)

    def pair_arrival(i):
        remote(tr.at[i], wt.at[c, 1 - half, i], y_send.at[i], y_recv.at[i], pair).wait_recv()

    def mate_copy(core, h, i):
        return remote(wt.at[core, h, i], wt.at[core, h, i], c_send.at[h, i], c_recv.at[h, i], mate)

    def when_chunk(i, body):
        @pl.when((i >= 0) & (i < NC))
        def _():
            body(i)

    def tick(t):
        def on_m(i):
            m_pass(i)
            mate_copy(c, half, i).start()

        def on_o(i):
            o_pass(i)
            pair_copy(i).start()

        def on_y(i):
            pair_arrival(i)
            mate_copy(c, 1 - half, i).start()

        when_chunk(t - LAG * m_far, on_m)
        when_chunk(t - LAG * o_far, on_o)
        when_chunk(t - LAG * m_far - 3, on_y)

        @pl.when(t == 0)
        def _():
            mine.wait()
            loop(3, lambda n: x_copy(0, n).start())

        @pl.when(t == 6)
        def _():
            def second(k):
                sy = lax.rem(y + 3 - k, 4)
                remote(xs.at[sy], rx.at[x, sy], ry_send.at[k], ry_recv.at[k], pair).wait_recv()
                loop(3, lambda n: x_copy(k + 1, n).start())

            loop(3, second)

    loop(NC + 8 * LAG + 3, tick)

    def mate_arrival(i):
        mate_copy(1 - c, 0, i).wait_recv()
        mate_copy(1 - c, 1, i).wait_recv()

    loop(NC, mate_arrival)
    loop(4, lambda k: loop(3, lambda n: x_arrival(k, n)))

    def part_copy(i):
        px, py = plane(i)
        return remote(pb.at[px, py], out.at[x, y], p_send.at[i], p_recv.at[i], dev(px, py, z, c))

    def hidden_copy(g, i):
        sx = lax.rem(x + g, 4)
        sy = i // 4
        s = lax.rem(i // 2, 2)
        turn = lax.rem(i, 2)
        dz = lax.rem(4 * expert + 2 * xl + s + 8 * turn, 16)
        dx = 2 * xh + lax.rem(sx, 2)
        q = z * 2 + sx // 2
        same = (dx == x) & (sy == y) & (dz == z)
        src = hs.at[sx, sy, :, pl.ds(pl.multiple_of(HS * s, HS), HS)]
        return same, turn, q, src, dev(dx, sy, dz, c)

    def send_hidden(g, i):
        same, turn, q, src, target = hidden_copy(g, i)
        for k, (dst, recv) in enumerate(((ha, ha_recv), (hb, hb_recv))):
            @pl.when((turn == k) & same)
            def _():
                pltpu.make_async_copy(src, dst.at[q], recv.at[q]).start()

            @pl.when((turn == k) & jnp.logical_not(same))
            def _():
                remote(src, dst.at[q], h_send.at[g, i], recv.at[q], target).start()

    def sent_hidden(g, i):
        same, turn, q, src, target = hidden_copy(g, i)

        @pl.when(jnp.logical_not(same))
        def _():
            remote(src, ha.at[q], h_send.at[g, i], ha_recv.at[q], target).wait_send()

    def group(step):
        g = lax.rem(step + 1, 4)
        sx = lax.rem(x + g, 4)
        block = rx[sx].reshape(4 * CAP, D)
        parts = []
        for s in range(2):
            gate_up = jnp.dot(block[:, :DH], wt[s, 0, 0:NI].reshape(DH, 2 * HS), preferred_element_type=F32)
            gate_up += jnp.dot(block[:, DH:], wt[s, 1, 0:NI].reshape(DH, 2 * HS), preferred_element_type=F32)
            v, u = gate_up[:, :HS], gate_up[:, HS:]
            parts.append((v / (1.0 + jnp.exp(-v)) * u).astype(BF))
        hs[sx] = jnp.concatenate(parts, axis=1).reshape(4, CAP, 2 * HS)
        for n in range(14):
            partial = jnp.dot(parts[0], wt[0, n % 2, NI + n // 2], preferred_element_type=F32)
            partial += jnp.dot(parts[1], wt[1, n % 2, NI + n // 2], preferred_element_type=F32)
            pb[sx, :, :, pl.ds(n * 256, 256)] = partial.astype(BF).reshape(4, CAP, 256)

        def leave(k):
            i = 4 * g + k

            @pl.when(i > 0)
            def _():
                part_copy(i).start()

        loop(4, leave)
        loop(16, lambda i: send_hidden(g, i))

    loop(4, group)
    own = pltpu.make_async_copy(pb.at[x, y], out.at[x, y], loc.at[3])
    own.start()

    def hidden_arrival(q):
        pltpu.make_async_copy(ha.at[q], ha.at[q], ha_recv.at[q]).wait()
        pltpu.make_async_copy(hb.at[q], hb.at[q], hb_recv.at[q]).wait()

    loop(32, hidden_arrival)
    flag = swap[lax.rem(ep, 16)]
    saved[...] = jnp.where(flag == 1, hb[...], ha[...])

    own.wait()

    def part_arrival(i):
        k = i + 1
        px, py = lax.rem(x + 4 - k // 4, 4), lax.rem(y + 4 - lax.rem(k, 4), 4)
        remote(pb.at[px, py], out.at[px, py], p_send.at[k], p_recv.at[k], dev(px, py, z, c)).wait_recv()

    loop(15, part_arrival)
    for n in range(7):
        cols = pl.ds(n * 512, 512)
        total = out[0, :, :, cols].astype(F32)
        for k in range(1, 4):
            total = total + out[k, :, :, cols].astype(F32)
        mixed[:, cols] = jnp.dot(
            gmat[...], total.reshape(4 * CAP, 512),
            precision=lax.Precision.HIGHEST, preferred_element_type=F32,
        ).astype(BF)

    loop(3, lambda k: y_copy(k).wait_send())
    loop(4, lambda k: loop(3, lambda n: x_copy(k, n).wait_send()))
    loop(15, lambda i: part_copy(i + 1).wait_send())
    loop(64, lambda i: sent_hidden(i // 16, lax.rem(i, 16)))
    m_settle()
    o_settle()
    loop(NC, lambda i: pair_copy(i).wait_send())

    def mate_sent(i):
        mate_copy(c, 0, i).wait_send()
        mate_copy(c, 1, i).wait_send()

    loop(NC, mate_sent)


def shards(tokens, route_token, route_expert, route_gate, w_in, w_out, swap_pairs):
    rows = route_token.shape[0]
    vmem = pl.BlockSpec(memory_space=pltpu.VMEM)
    hbm = pl.BlockSpec(memory_space=pl.ANY)
    dma = pltpu.SemaphoreType.DMA
    mixed, saved = pl.pallas_call(
        kernel,
        out_shape=(
            jax.ShapeDtypeStruct((128, D), BF),
            jax.ShapeDtypeStruct((32, CAP, HS), BF),
        ),
        in_specs=[vmem, vmem, vmem, vmem, vmem, pl.BlockSpec(memory_space=pltpu.SMEM), hbm, hbm],
        out_specs=(vmem, vmem),
        scratch_shapes=[
            pltpu.VMEM((4, CAP, D), BF),
            pltpu.VMEM((4, 4, CAP, D), BF),
            pltpu.VMEM((4, 4, CAP, D), BF),
            pltpu.VMEM((4, 4, CAP, 2 * HS), BF),
            pltpu.VMEM((4, 4, CAP, D), BF),
            pltpu.VMEM((32, CAP, HS), BF),
            pltpu.VMEM((32, CAP, HS), BF),
            pltpu.VMEM((2, 2, NC, 128, 256), BF),
            pltpu.VMEM((NC, 128, 256), BF),
            pltpu.VMEM((128, 4 * CAP), F32),
            dma((3,)), dma((3,)), dma((4, 3)), dma((4, 3)), dma((16,)), dma((16,)), dma((4, 16)), dma((32,)), dma((32,)),
            dma((NC,)), dma((NC,)), dma((NC,)), dma((NC,)), dma((NC,)), dma((NC,)), dma((NC,)), dma((NC,)),
            dma((2, NC)), dma((2, NC)), dma((NC,)),
            dma((4,)),
        ],
        compiler_params=pltpu.CompilerParams(
            collective_id=0, has_side_effects=True, vmem_limit_bytes=60 * 1024 * 1024
        ),
    )(
        tokens,
        route_token.reshape(1, rows),
        route_expert.reshape(1, rows),
        route_expert,
        route_gate.reshape(1, rows),
        swap_pairs,
        w_in[0],
        w_out[0],
    )
    return mixed, saved.reshape(1, 32 * CAP, HS)


def solution(mesh):
    return jax.shard_map(
        shards,
        mesh=mesh,
        in_specs=(
            P(("rep", "ep"), None),
            P(("rep", "ep")),
            P(("rep", "ep"), None),
            P(("rep", "ep")),
            P("ep", None, None),
            P("ep", None, None),
            P(),
        ),
        out_specs=(P(("rep", "ep"), None), P(("rep", "ep"), None, None)),
        check_vma=False,
    )
```

```python
import jax
import jax.numpy as jnp
from jax import lax
from jax.experimental import pallas as pl
from jax.experimental.pallas import tpu as pltpu
from jax.sharding import PartitionSpec as P

MESH = pl.DeviceIdType.MESH
BF = jnp.bfloat16
F32 = jnp.float32
CAP = 24
D = 3584
HS = 128
DH = D // 2
NI = 14
NO = 7
NC = NI + NO
LAG = 3


def loop(n, body):
    def step(i, carry):
        body(i)
        return carry

    lax.fori_loop(0, n, step, 0)


def kernel(
    tokens, tok_row, exp_row, exp_col, gate_row, swap, w_in, w_out,
    mixed, saved,
    xs, rx, pb, hs, hp, hq, rl, fa, fb, sb, out, ha, wt, tr, gmat,
    ry_send, ry_recv, rx_send, rx_recv, l_send, l_recv, a_send, a_recv, b_send, b_recv, s_send, s_recv, h_send, h_recv, hp_send, hp_recv,
    m_up, m_down, m_recv, o_up, o_down, o_recv, y_send, y_recv, c_send, c_recv, seed, loc,
):
    rep = lax.axis_index("rep")
    ep = lax.axis_index("ep")
    c = lax.rem(rep, 2)
    y = lax.rem(rep // 2, 4)
    xl = rep // 8
    xh = lax.rem(ep, 2)
    z = ep // 2
    x = 2 * xh + xl

    def dev(dx, dy, dz, dc):
        return ((lax.rem(dx, 2) * 4 + dy) * 2 + dc, dz * 2 + dx // 2)

    def swapped(v):
        return v // 2 + 2 * lax.rem(v, 2)

    expert = swapped(y)
    half = lax.rem(y, 2)
    mate = dev(x, y, z, 1 - c)
    pair = dev(x, y + 1 - 2 * half, z, c)
    above = dev(x, y, lax.rem(z + 1, 16), c)
    below = dev(x, y, lax.rem(z + 15, 16), c)
    m_at = lax.rem(z - (4 * expert + 2 * xl + c) + 32, 16)
    o_at = lax.rem(m_at + 8, 16)

    barrier = pltpu.get_barrier_semaphore()

    def greet(target):
        pl.semaphore_signal(barrier, inc=1, device_id=target, device_id_type=MESH)

    unit = lax.rem(z, 4)

    def greet_column(i):
        dx = 2 * xh + unit // 2
        dy = swapped(z // 4)
        same = (dx == x) & (dy == y) & (i == z)

        @pl.when(jnp.logical_not(same))
        def _():
            greet(dev(dx, dy, i, c))

    loop(16, greet_column)

    def greet_rings(i):
        greet(dev(lax.rem(x + i + 1, 4), y, z, c))
        greet(dev(x, lax.rem(y + i + 1, 4), z, c))

    loop(3, greet_rings)
    greet(above)
    greet(below)
    greet(mate)
    own_a = ((unit // 2 == xl) & (swapped(z // 4) == y)).astype(jnp.int32)

    own_half = wt.at[c, half]

    def seed_copy(i, dst, act):
        @pl.when(i < NI)
        def _():
            rows_at = pl.ds(pl.multiple_of(DH * half + 128 * i, 128), 128)
            act(pltpu.make_async_copy(w_in.at[rows_at], dst.at[i], seed.at[i]))

        @pl.when(i >= NI)
        def _():
            cols_at = pl.ds(pl.multiple_of(256 * (2 * (i - NI) + half), 256), 256)
            act(pltpu.make_async_copy(w_out.at[:, cols_at], dst.at[i], seed.at[i]))

    for at, dst in ((m_at, own_half), (o_at, tr)):
        @pl.when(at == 0)
        def _():
            loop(NC, lambda i: seed_copy(i, dst, lambda d: d.start()))

    rows = exp_row.shape[1]
    earlier = (exp_col[...] == exp_row[...]) & (
        lax.broadcasted_iota(jnp.int32, (rows, rows), 0)
        < lax.broadcasted_iota(jnp.int32, (rows, rows), 1)
    )
    slot = jnp.sum(earlier.astype(F32), axis=0, keepdims=True).astype(jnp.int32)
    line = lax.shift_right_logical(exp_row[...], 1) + 2 * (exp_row[...] & 1)
    key = line * CAP + slot
    tok_hot = (lax.broadcasted_iota(jnp.int32, (128, rows), 0) == tok_row[...]).astype(F32)
    contract = (((1,), (1,)), ((), ()))
    place_all = (lax.broadcasted_iota(jnp.int32, (4 * CAP, rows), 0) == key).astype(F32)
    gmat[...] = lax.dot_general(
        tok_hot * gate_row[...], place_all, contract,
        precision=lax.Precision.HIGHEST, preferred_element_type=F32,
    )
    for e in range(4):
        place = (lax.broadcasted_iota(jnp.int32, (CAP, rows), 0) + CAP * e == key).astype(BF)
        pick = lax.dot_general(place, tok_hot.astype(BF), contract, preferred_element_type=F32).astype(BF)
        for n in range(7):
            cols = pl.ds(n * 512, 512)
            xs[e, :, cols] = jnp.dot(pick, tokens[:, cols], preferred_element_type=F32).astype(BF)

    pl.semaphore_wait(barrier, 25 - own_a)

    def remote(src, dst, send, recv, target):
        return pltpu.make_async_remote_copy(
            src_ref=src, dst_ref=dst, send_sem=send, recv_sem=recv,
            device_id=target, device_id_type=MESH,
        )

    def y_copy(k):
        py = lax.rem(y + k + 1, 4)
        return remote(xs.at[py], rx.at[x, y], ry_send.at[k], ry_recv.at[k], dev(x, py, z, c))

    def x_copy(k, n):
        sy = lax.rem(y + 4 - k, 4)
        return remote(
            rx.at[x, sy], rx.at[x, sy], rx_send.at[k, n], rx_recv.at[k, n],
            dev(lax.rem(x + n + 1, 4), y, z, c),
        )

    def x_arrival(k, n):
        sx, sy = lax.rem(x + 3 - n, 4), lax.rem(y + 4 - k, 4)
        remote(rx.at[sx, sy], rx.at[sx, sy], rx_send.at[k, n], rx_recv.at[k, n], pair).wait_recv()

    loop(3, lambda k: y_copy(k).start())
    mine = pltpu.make_async_copy(xs.at[y], rx.at[x, y], loc.at[2])
    mine.start()

    def stream(buf, at, up, down, recv):
        far = jnp.where(at > 8, 16 - at, at)
        goes_up = at <= 7
        goes_down = (at == 0) | (at >= 10)

        def to_above(i):
            return remote(buf.at[i], buf.at[i], up.at[i], recv.at[i], above)

        def to_below(i):
            return remote(buf.at[i], buf.at[i], down.at[i], recv.at[i], below)

        def pass_on(i):
            @pl.when(at != 0)
            def _():
                to_above(i).wait_recv()

            @pl.when(at == 0)
            def _():
                seed_copy(i, buf, lambda d: d.wait())

            @pl.when(goes_up)
            def _():
                to_above(i).start()

            @pl.when(goes_down)
            def _():
                to_below(i).start()

        def settle():
            @pl.when(goes_up)
            def _():
                loop(NC, lambda i: to_above(i).wait_send())

            @pl.when(goes_down)
            def _():
                loop(NC, lambda i: to_below(i).wait_send())

        return far, pass_on, settle

    m_far, m_pass, m_settle = stream(own_half, m_at, m_up, m_down, m_recv)
    o_far, o_pass, o_settle = stream(tr, o_at, o_up, o_down, o_recv)

    def pair_copy(i):
        return remote(tr.at[i], wt.at[c, half, i], y_send.at[i], y_recv.at[i], pair)

    def pair_arrival(i):
        remote(tr.at[i], wt.at[c, 1 - half, i], y_send.at[i], y_recv.at[i], pair).wait_recv()

    def mate_copy(core, h, i):
        return remote(wt.at[core, h, i], wt.at[core, h, i], c_send.at[h, i], c_recv.at[h, i], mate)

    def when_chunk(i, body):
        @pl.when((i >= 0) & (i < NC))
        def _():
            body(i)

    def mate_arrival(i):
        mate_copy(1 - c, 0, i).wait_recv()
        mate_copy(1 - c, 1, i).wait_recv()

    def activate(sx):
        block = rx[sx].reshape(4 * CAP, D)
        for s in range(2):
            gate_up = jnp.dot(block[:, :DH], wt[s, 0, 0:NI].reshape(DH, 2 * HS), preferred_element_type=F32)
            gate_up += jnp.dot(block[:, DH:], wt[s, 1, 0:NI].reshape(DH, 2 * HS), preferred_element_type=F32)
            v, u = gate_up[:, :HS], gate_up[:, HS:]
            act = (v / (1.0 + jnp.exp(-v)) * u).astype(BF).reshape(4, CAP, HS)
            for sy in range(4):
                hs[lax.rem(sx, 2), sy, s, sx // 2] = act[sy]

    ready_at = jnp.maximum(LAG * m_far + NI + 6, 32)
    hidden_swap = remote(hs, hp, hp_send.at[0], hp_recv.at[0], pair)

    def tick(t):
        def on_m(i):
            m_pass(i)
            mate_copy(c, half, i).start()

        def on_o(i):
            o_pass(i)
            pair_copy(i).start()

        def on_y(i):
            pair_arrival(i)
            mate_copy(c, 1 - half, i).start()

        when_chunk(t - LAG * m_far, on_m)
        when_chunk(t - LAG * o_far, on_o)
        when_chunk(t - LAG * m_far - 3, on_y)

        @pl.when(t == ready_at)
        def _():
            loop(NI, mate_arrival)
            loop(4, lambda k: loop(3, lambda n: x_arrival(k, n)))
            loop(4, activate)
            hidden_swap.start()

        @pl.when(t == 0)
        def _():
            mine.wait()
            loop(3, lambda n: x_copy(0, n).start())

        @pl.when(t == 6)
        def _():
            def second(k):
                sy = lax.rem(y + 3 - k, 4)
                remote(xs.at[sy], rx.at[x, sy], ry_send.at[k], ry_recv.at[k], pair).wait_recv()
                loop(3, lambda n: x_copy(k + 1, n).start())

            loop(3, second)

    loop(NC + 8 * LAG + 3, tick)

    loop(NO, lambda i: mate_arrival(NI + i))

    def hidden_copy(i):
        lo, sy, s = i // 8, lax.rem(i // 2, 4), lax.rem(i, 2)
        dz = 4 * expert + 2 * xl + s
        same = (lo == xl) & (sy == y) & (dz == z)
        return same, hq.at[lo, sy, s], dev(2 * xh + lo, sy, dz, c)

    kept = pl.ds(2 * z, 2)

    def send_hidden(i):
        same, src, target = hidden_copy(i)

        @pl.when(same)
        def _():
            pltpu.make_async_copy(src, ha.at[kept], h_recv.at[z]).start()

        @pl.when(jnp.logical_not(same))
        def _():
            remote(src, ha.at[kept], h_send.at[i], h_recv.at[z], target).start()

    def sent_hidden(i):
        same, src, target = hidden_copy(i)

        @pl.when(jnp.logical_not(same))
        def _():
            remote(src, ha.at[kept], h_send.at[i], h_recv.at[z], target).wait_send()

    def match_hidden():
        hidden_swap.wait_recv()
        for s in range(2):
            flag = swap[lax.rem(2 * (4 * expert + 2 * xl + s) + xh, 16)]
            hq[:, :, s] = jnp.where(flag == 1, hp[:, :, s], hs[:, :, s])
        loop(16, send_hidden)

    ring_up = dev(lax.rem(x + 1, 4), y, z, c)
    ring_down = dev(lax.rem(x + 3, 4), y, z, c)
    far_x, up_x, down_x = lax.rem(x + 2, 4), lax.rem(x + 1, 4), lax.rem(x + 3, 4)

    def row_of(k):
        return lax.rem(y + k, 4)

    def partials(sx):
        parts = [
            jnp.concatenate([hs[lax.rem(sx, 2), sy, s, sx // 2] for sy in range(4)], axis=0)
            for s in range(2)
        ]
        for n in range(14):
            partial = jnp.dot(parts[0], wt[0, n % 2, NI + n // 2], preferred_element_type=F32)
            partial += jnp.dot(parts[1], wt[1, n % 2, NI + n // 2], preferred_element_type=F32)
            pb[sx, :, :, pl.ds(n * 256, 256)] = partial.astype(BF).reshape(4, CAP, 256)

    def relay_up(k):
        return remote(pb.at[far_x, row_of(k)], rl.at[k], l_send.at[k], l_recv.at[k], ring_up)

    def relay_down(k):
        return remote(pb.at[far_x, row_of(k)], rl.at[k], l_send.at[k], l_recv.at[k], ring_down)

    def to_up(k):
        return remote(pb.at[up_x, row_of(k)], fa.at[k], a_send.at[k], a_recv.at[k], ring_up)

    def to_down(k):
        return remote(pb.at[down_x, row_of(k)], fb.at[k], b_send.at[k], b_recv.at[k], ring_down)

    def home(k):
        return remote(sb.at[k], out.at[y], s_send.at[k], s_recv.at[k], dev(x, row_of(k), z, c))

    def stage(g):
        partials(lax.rem(x + g, 4))

        @pl.when(g == 2)
        def _():
            relay_down(2).start()
            relay_up(1).start()
            relay_down(3).start()
            relay_up(0).start()

        @pl.when(g == 1)
        def _():
            to_up(2).start()
            to_up(3).start()

        @pl.when(g == 3)
        def _():
            to_down(1).start()
            to_down(0).start()
            match_hidden()

    loop(4, lambda i: stage(jnp.where(i == 0, 2, jnp.where(i == 1, 1, jnp.where(i == 2, 3, 0)))))

    def add_up(k):
        relay_up(k).wait_recv()
        row = row_of(k)
        pb[up_x, row] = (pb[up_x, row].astype(F32) + rl[k].astype(F32)).astype(BF)
        to_up(k).start()

    def add_down(k):
        relay_down(k).wait_recv()
        row = row_of(k)
        pb[down_x, row] = (pb[down_x, row].astype(F32) + rl[k].astype(F32)).astype(BF)
        to_down(k).start()

    def adds(i):
        add_down(2 + i)
        add_up(1 - i)

    loop(2, adds)

    def finish(i):
        k = jnp.where(i == 0, 2, jnp.where(i == 1, 1, jnp.where(i == 2, 3, 0)))
        to_up(k).wait_recv()
        to_down(k).wait_recv()
        total = pb[x, row_of(k)].astype(F32) + fa[k].astype(F32) + fb[k].astype(F32)

        @pl.when(k > 0)
        def _():
            sb[k] = total.astype(BF)
            home(k).start()

        @pl.when(k == 0)
        def _():
            out[y] = total.astype(BF)

    loop(4, finish)

    def hidden_arrival(q):
        pair_of = pl.ds(2 * q, 2)
        pltpu.make_async_copy(ha.at[pair_of], ha.at[pair_of], h_recv.at[q]).wait()

    loop(16, hidden_arrival)
    saved[...] = ha[...]

    def home_arrival(k):
        remote(sb.at[k], out.at[lax.rem(y + 4 - k, 4)], s_send.at[k], s_recv.at[k], pair).wait_recv()

    loop(3, lambda k: home_arrival(k + 1))
    for n in range(7):
        cols = pl.ds(n * 512, 512)
        mixed[:, cols] = jnp.dot(
            gmat[...], out[:, :, cols].astype(F32).reshape(4 * CAP, 512),
            precision=lax.Precision.HIGHEST, preferred_element_type=F32,
        ).astype(BF)

    loop(3, lambda k: y_copy(k).wait_send())
    loop(4, lambda k: loop(3, lambda n: x_copy(k, n).wait_send()))

    def ring_sent(k):
        relay_up(k).wait_send()
        to_up(k).wait_send()
        to_down(k).wait_send()

    loop(4, ring_sent)
    loop(3, lambda k: home(k + 1).wait_send())
    loop(16, sent_hidden)
    hidden_swap.wait_send()
    m_settle()
    o_settle()
    loop(NC, lambda i: pair_copy(i).wait_send())

    def mate_sent(i):
        mate_copy(c, 0, i).wait_send()
        mate_copy(c, 1, i).wait_send()

    loop(NC, mate_sent)


def shards(tokens, route_token, route_expert, route_gate, w_in, w_out, swap_pairs):
    rows = route_token.shape[0]
    vmem = pl.BlockSpec(memory_space=pltpu.VMEM)
    hbm = pl.BlockSpec(memory_space=pl.ANY)
    dma = pltpu.SemaphoreType.DMA
    mixed, saved = pl.pallas_call(
        kernel,
        out_shape=(
            jax.ShapeDtypeStruct((128, D), BF),
            jax.ShapeDtypeStruct((32, CAP, HS), BF),
        ),
        in_specs=[vmem, vmem, vmem, vmem, vmem, pl.BlockSpec(memory_space=pltpu.SMEM), hbm, hbm],
        out_specs=(vmem, vmem),
        scratch_shapes=[
            pltpu.VMEM((4, CAP, D), BF),
            pltpu.VMEM((4, 4, CAP, D), BF),
            pltpu.VMEM((4, 4, CAP, D), BF),
            pltpu.VMEM((2, 4, 2, 2, CAP, HS), BF),
            pltpu.VMEM((2, 4, 2, 2, CAP, HS), BF),
            pltpu.VMEM((2, 4, 2, 2, CAP, HS), BF),
            pltpu.VMEM((4, CAP, D), BF),
            pltpu.VMEM((4, CAP, D), BF),
            pltpu.VMEM((4, CAP, D), BF),
            pltpu.VMEM((4, CAP, D), BF),
            pltpu.VMEM((4, CAP, D), BF),
            pltpu.VMEM((32, CAP, HS), BF),
            pltpu.VMEM((2, 2, NC, 128, 256), BF),
            pltpu.VMEM((NC, 128, 256), BF),
            pltpu.VMEM((128, 4 * CAP), F32),
            dma((3,)), dma((3,)), dma((4, 3)), dma((4, 3)), dma((4,)), dma((4,)), dma((4,)), dma((4,)), dma((4,)), dma((4,)), dma((4,)), dma((4,)),
            dma((16,)), dma((16,)), dma((1,)), dma((1,)),
            dma((NC,)), dma((NC,)), dma((NC,)), dma((NC,)), dma((NC,)), dma((NC,)), dma((NC,)), dma((NC,)),
            dma((2, NC)), dma((2, NC)), dma((NC,)),
            dma((4,)),
        ],
        compiler_params=pltpu.CompilerParams(
            collective_id=0, has_side_effects=True, vmem_limit_bytes=60 * 1024 * 1024
        ),
    )(
        tokens,
        route_token.reshape(1, rows),
        route_expert.reshape(1, rows),
        route_expert,
        route_gate.reshape(1, rows),
        swap_pairs,
        w_in[0],
        w_out[0],
    )
    return mixed, saved.reshape(1, 32 * CAP, HS)


def solution(mesh):
    return jax.shard_map(
        shards,
        mesh=mesh,
        in_specs=(
            P(("rep", "ep"), None),
            P(("rep", "ep")),
            P(("rep", "ep"), None),
            P(("rep", "ep")),
            P("ep", None, None),
            P("ep", None, None),
            P(),
        ),
        out_specs=(P(("rep", "ep"), None), P(("rep", "ep"), None, None)),
        check_vma=False,
    )
```

```python
import jax
import jax.numpy as jnp
from jax import lax
from jax.experimental import pallas as pl
from jax.experimental.pallas import tpu as pltpu
from jax.sharding import PartitionSpec as P

MESH = pl.DeviceIdType.MESH
BF = jnp.bfloat16
F32 = jnp.float32
CAP = 24
D = 3584
HS = 128
DH = D // 2
NI = 14
NO = 7
NC = NI + NO
LAG = 3


def loop(n, body):
    def step(i, carry):
        body(i)
        return carry

    lax.fori_loop(0, n, step, 0)


def kernel(
    tokens, tok_row, exp_row, exp_col, gate_row, swap, w_in, w_out,
    mixed, saved,
    xs, rx, pb, hs, hp, hq, hz, rl, fa, fb, sb, out, ha, wt, tr, gmat,
    ry_send, ry_recv, rx_send, rx_recv, l_send, l_recv, a_send, a_recv, b_send, b_recv, s_send, s_recv, g_send, g_recv, h_send, h_recv, hp_send, hp_recv,
    m_up, m_down, m_recv, o_up, o_down, o_recv, y_send, y_recv, c_send, c_recv, seed, loc,
):
    rep = lax.axis_index("rep")
    ep = lax.axis_index("ep")
    c = lax.rem(rep, 2)
    y = lax.rem(rep // 2, 4)
    xl = rep // 8
    xh = lax.rem(ep, 2)
    z = ep // 2
    x = 2 * xh + xl

    def dev(dx, dy, dz, dc):
        return ((lax.rem(dx, 2) * 4 + dy) * 2 + dc, dz * 2 + dx // 2)

    def swapped(v):
        return v // 2 + 2 * lax.rem(v, 2)

    expert = swapped(y)
    half = lax.rem(y, 2)
    mate = dev(x, y, z, 1 - c)
    pair = dev(x, y + 1 - 2 * half, z, c)
    above = dev(x, y, lax.rem(z + 1, 16), c)
    below = dev(x, y, lax.rem(z + 15, 16), c)
    m_at = lax.rem(z - (4 * expert + 2 * xl + c) + 32, 16)
    o_at = lax.rem(m_at + 8, 16)

    barrier = pltpu.get_barrier_semaphore()

    def greet(target):
        pl.semaphore_signal(barrier, inc=1, device_id=target, device_id_type=MESH)

    def beside(i):
        return i // 4, lax.rem(y + i, 4)

    def greet_column(i):
        @pl.when(i != z)
        def _():
            greet(dev(x, y, i, c))

    def greet_beside(i):
        lo, py = beside(i)

        @pl.when((lo != xl) | (py != y))
        def _():
            greet(dev(2 * xh + lo, py, z, c))

    loop(16, greet_column)
    loop(8, greet_beside)
    loop(3, lambda i: greet(dev(lax.rem(x + i + 1, 4), y, z, c)))
    greet(above)
    greet(below)
    greet(mate)

    own_half = wt.at[c, half]

    def seed_copy(i, dst, act):
        @pl.when(i < NI)
        def _():
            rows_at = pl.ds(pl.multiple_of(DH * half + 128 * i, 128), 128)
            act(pltpu.make_async_copy(w_in.at[rows_at], dst.at[i], seed.at[i]))

        @pl.when(i >= NI)
        def _():
            cols_at = pl.ds(pl.multiple_of(256 * (2 * (i - NI) + half), 256), 256)
            act(pltpu.make_async_copy(w_out.at[:, cols_at], dst.at[i], seed.at[i]))

    for at, dst in ((m_at, own_half), (o_at, tr)):
        @pl.when(at == 0)
        def _():
            loop(NC, lambda i: seed_copy(i, dst, lambda d: d.start()))

    rows = exp_row.shape[1]
    earlier = (exp_col[...] == exp_row[...]) & (
        lax.broadcasted_iota(jnp.int32, (rows, rows), 0)
        < lax.broadcasted_iota(jnp.int32, (rows, rows), 1)
    )
    slot = jnp.sum(earlier.astype(F32), axis=0, keepdims=True).astype(jnp.int32)
    line = lax.shift_right_logical(exp_row[...], 1) + 2 * (exp_row[...] & 1)
    key = line * CAP + slot
    tok_hot = (lax.broadcasted_iota(jnp.int32, (128, rows), 0) == tok_row[...]).astype(F32)
    contract = (((1,), (1,)), ((), ()))
    place_all = (lax.broadcasted_iota(jnp.int32, (4 * CAP, rows), 0) == key).astype(F32)
    gmat[...] = lax.dot_general(
        tok_hot * gate_row[...], place_all, contract,
        precision=lax.Precision.HIGHEST, preferred_element_type=F32,
    )
    for e in range(4):
        place = (lax.broadcasted_iota(jnp.int32, (CAP, rows), 0) + CAP * e == key).astype(BF)
        pick = lax.dot_general(place, tok_hot.astype(BF), contract, preferred_element_type=F32).astype(BF)
        for n in range(7):
            cols = pl.ds(n * 512, 512)
            xs[e, :, cols] = jnp.dot(pick, tokens[:, cols], preferred_element_type=F32).astype(BF)

    pl.semaphore_wait(barrier, 28)

    def remote(src, dst, send, recv, target):
        return pltpu.make_async_remote_copy(
            src_ref=src, dst_ref=dst, send_sem=send, recv_sem=recv,
            device_id=target, device_id_type=MESH,
        )

    def y_copy(k):
        py = lax.rem(y + k + 1, 4)
        return remote(xs.at[py], rx.at[x, y], ry_send.at[k], ry_recv.at[k], dev(x, py, z, c))

    def x_copy(k, n):
        sy = lax.rem(y + 4 - k, 4)
        return remote(
            rx.at[x, sy], rx.at[x, sy], rx_send.at[k, n], rx_recv.at[k, n],
            dev(lax.rem(x + n + 1, 4), y, z, c),
        )

    def x_arrival(k, n):
        sx, sy = lax.rem(x + 3 - n, 4), lax.rem(y + 4 - k, 4)
        remote(rx.at[sx, sy], rx.at[sx, sy], rx_send.at[k, n], rx_recv.at[k, n], pair).wait_recv()

    loop(3, lambda k: y_copy(k).start())
    mine = pltpu.make_async_copy(xs.at[y], rx.at[x, y], loc.at[2])
    mine.start()

    def stream(buf, at, up, down, recv):
        far = jnp.where(at > 8, 16 - at, at)
        goes_up = at <= 7
        goes_down = (at == 0) | (at >= 10)

        def to_above(i):
            return remote(buf.at[i], buf.at[i], up.at[i], recv.at[i], above)

        def to_below(i):
            return remote(buf.at[i], buf.at[i], down.at[i], recv.at[i], below)

        def pass_on(i):
            @pl.when(at != 0)
            def _():
                to_above(i).wait_recv()

            @pl.when(at == 0)
            def _():
                seed_copy(i, buf, lambda d: d.wait())

            @pl.when(goes_up)
            def _():
                to_above(i).start()

            @pl.when(goes_down)
            def _():
                to_below(i).start()

        def settle():
            @pl.when(goes_up)
            def _():
                loop(NC, lambda i: to_above(i).wait_send())

            @pl.when(goes_down)
            def _():
                loop(NC, lambda i: to_below(i).wait_send())

        return far, pass_on, settle

    m_far, m_pass, m_settle = stream(own_half, m_at, m_up, m_down, m_recv)
    o_far, o_pass, o_settle = stream(tr, o_at, o_up, o_down, o_recv)

    def pair_copy(i):
        return remote(tr.at[i], wt.at[c, half, i], y_send.at[i], y_recv.at[i], pair)

    def pair_arrival(i):
        remote(tr.at[i], wt.at[c, 1 - half, i], y_send.at[i], y_recv.at[i], pair).wait_recv()

    def mate_copy(core, h, i):
        return remote(wt.at[core, h, i], wt.at[core, h, i], c_send.at[h, i], c_recv.at[h, i], mate)

    def when_chunk(i, body):
        @pl.when((i >= 0) & (i < NC))
        def _():
            body(i)

    def mate_arrival(i):
        mate_copy(1 - c, 0, i).wait_recv()
        mate_copy(1 - c, 1, i).wait_recv()

    def activate(sx):
        block = rx[sx].reshape(4 * CAP, D)
        for s in range(2):
            gate_up = jnp.dot(block[:, :DH], wt[s, 0, 0:NI].reshape(DH, 2 * HS), preferred_element_type=F32)
            gate_up += jnp.dot(block[:, DH:], wt[s, 1, 0:NI].reshape(DH, 2 * HS), preferred_element_type=F32)
            v, u = gate_up[:, :HS], gate_up[:, HS:]
            act = (v / (1.0 + jnp.exp(-v)) * u).astype(BF).reshape(4, CAP, HS)
            for sy in range(4):
                hs[lax.rem(sx, 2), sy, s, sx // 2] = act[sy]

    ready_at = jnp.maximum(LAG * m_far + NI + 6, 32)
    hidden_swap = remote(hs, hp, hp_send.at[0], hp_recv.at[0], pair)

    first_slice = 4 * expert + 2 * xl

    def spread_copy(i):
        lo, sy = beside(i)
        src, dst = hq.at[lo, sy], hz.at[pl.ds(first_slice, 2)]
        return (lo == xl) & (sy == y), src, dst, dev(2 * xh + lo, sy, z, c)

    def spread_hidden(i):
        same, src, dst, target = spread_copy(i)

        @pl.when(same)
        def _():
            pltpu.make_async_copy(src, dst, g_recv.at[first_slice // 2]).start()

        @pl.when(jnp.logical_not(same))
        def _():
            remote(src, dst, g_send.at[i], g_recv.at[first_slice // 2], target).start()

    def spread_sent(i):
        same, src, dst, target = spread_copy(i)

        @pl.when(jnp.logical_not(same))
        def _():
            remote(src, dst, g_send.at[i], g_recv.at[first_slice // 2], target).wait_send()

    kept = pl.ds(2 * z, 2)

    def column_copy(i):
        return remote(hz.at[i], ha.at[kept], h_send.at[i], h_recv.at[z], dev(x, y, i, c))

    def send_column(i):
        @pl.when(i == z)
        def _():
            pltpu.make_async_copy(hz.at[i], ha.at[kept], h_recv.at[z]).start()

        @pl.when(i != z)
        def _():
            column_copy(i).start()

    def column_sent(i):
        @pl.when(i != z)
        def _():
            column_copy(i).wait_send()

    def forward_hidden():
        def both(n):
            piece = hz.at[pl.ds(2 * n, 2)]
            pltpu.make_async_copy(piece, piece, g_recv.at[n]).wait()
            send_column(2 * n)
            send_column(2 * n + 1)

        loop(8, both)

    def match_hidden():
        hidden_swap.wait_recv()
        for s in range(2):
            flag = swap[lax.rem(2 * (first_slice + s) + xh, 16)]
            hq[:, :, s] = jnp.where(flag == 1, hp[:, :, s], hs[:, :, s])
        loop(8, spread_hidden)

    match_at = jnp.maximum(LAG * jnp.maximum(m_far, o_far) + NI + 6, 32) + 3

    def tick(t):
        def on_m(i):
            m_pass(i)
            mate_copy(c, half, i).start()

        def on_o(i):
            o_pass(i)
            pair_copy(i).start()

        def on_y(i):
            pair_arrival(i)
            mate_copy(c, 1 - half, i).start()

        when_chunk(t - LAG * m_far, on_m)
        when_chunk(t - LAG * o_far, on_o)
        when_chunk(t - LAG * m_far - 3, on_y)

        @pl.when(t == ready_at)
        def _():
            loop(NI, mate_arrival)
            loop(4, lambda k: loop(3, lambda n: x_arrival(k, n)))
            loop(4, activate)
            hidden_swap.start()

        @pl.when(t == match_at)
        def _():
            match_hidden()

        @pl.when(t == 0)
        def _():
            mine.wait()
            loop(3, lambda n: x_copy(0, n).start())

        @pl.when(t == 6)
        def _():
            def second(k):
                sy = lax.rem(y + 3 - k, 4)
                remote(xs.at[sy], rx.at[x, sy], ry_send.at[k], ry_recv.at[k], pair).wait_recv()
                loop(3, lambda n: x_copy(k + 1, n).start())

            loop(3, second)

    loop(NC + 8 * LAG + 3, tick)

    loop(NO, lambda i: mate_arrival(NI + i))

    ring_up = dev(lax.rem(x + 1, 4), y, z, c)
    ring_down = dev(lax.rem(x + 3, 4), y, z, c)
    far_x, up_x, down_x = lax.rem(x + 2, 4), lax.rem(x + 1, 4), lax.rem(x + 3, 4)

    def row_of(k):
        return lax.rem(y + k, 4)

    def partials(sx):
        parts = [
            jnp.concatenate([hs[lax.rem(sx, 2), sy, s, sx // 2] for sy in range(4)], axis=0)
            for s in range(2)
        ]
        for n in range(14):
            partial = jnp.dot(parts[0], wt[0, n % 2, NI + n // 2], preferred_element_type=F32)
            partial += jnp.dot(parts[1], wt[1, n % 2, NI + n // 2], preferred_element_type=F32)
            pb[sx, :, :, pl.ds(n * 256, 256)] = partial.astype(BF).reshape(4, CAP, 256)

    def relay_up(k):
        return remote(pb.at[far_x, row_of(k)], rl.at[k], l_send.at[k], l_recv.at[k], ring_up)

    def relay_down(k):
        return remote(pb.at[far_x, row_of(k)], rl.at[k], l_send.at[k], l_recv.at[k], ring_down)

    def to_up(k):
        return remote(pb.at[up_x, row_of(k)], fa.at[k], a_send.at[k], a_recv.at[k], ring_up)

    def to_down(k):
        return remote(pb.at[down_x, row_of(k)], fb.at[k], b_send.at[k], b_recv.at[k], ring_down)

    def home(k):
        return remote(sb.at[k], out.at[y], s_send.at[k], s_recv.at[k], dev(x, row_of(k), z, c))

    def stage(g):
        partials(lax.rem(x + g, 4))

        @pl.when(g == 2)
        def _():
            relay_down(2).start()
            relay_up(1).start()
            relay_down(3).start()
            relay_up(0).start()

        @pl.when(g == 1)
        def _():
            to_up(2).start()
            to_up(3).start()

        @pl.when(g == 3)
        def _():
            to_down(1).start()
            to_down(0).start()
            forward_hidden()

    loop(4, lambda i: stage(jnp.where(i == 0, 2, jnp.where(i == 1, 1, jnp.where(i == 2, 3, 0)))))

    def add_up(k):
        relay_up(k).wait_recv()
        row = row_of(k)
        pb[up_x, row] = (pb[up_x, row].astype(F32) + rl[k].astype(F32)).astype(BF)
        to_up(k).start()

    def add_down(k):
        relay_down(k).wait_recv()
        row = row_of(k)
        pb[down_x, row] = (pb[down_x, row].astype(F32) + rl[k].astype(F32)).astype(BF)
        to_down(k).start()

    def adds(i):
        add_down(2 + i)
        add_up(1 - i)

    loop(2, adds)

    def finish(i):
        k = jnp.where(i == 0, 2, jnp.where(i == 1, 1, jnp.where(i == 2, 3, 0)))
        to_up(k).wait_recv()
        to_down(k).wait_recv()
        total = pb[x, row_of(k)].astype(F32) + fa[k].astype(F32) + fb[k].astype(F32)

        @pl.when(k > 0)
        def _():
            sb[k] = total.astype(BF)
            home(k).start()

        @pl.when(k == 0)
        def _():
            out[y] = total.astype(BF)

    loop(4, finish)

    def hidden_arrival(q):
        pair_of = pl.ds(2 * q, 2)
        pltpu.make_async_copy(ha.at[pair_of], ha.at[pair_of], h_recv.at[q]).wait()

    loop(16, hidden_arrival)
    saved[...] = ha[...]

    def home_arrival(k):
        remote(sb.at[k], out.at[lax.rem(y + 4 - k, 4)], s_send.at[k], s_recv.at[k], pair).wait_recv()

    loop(3, lambda k: home_arrival(k + 1))
    for n in range(7):
        cols = pl.ds(n * 512, 512)
        mixed[:, cols] = jnp.dot(
            gmat[...], out[:, :, cols].astype(F32).reshape(4 * CAP, 512),
            precision=lax.Precision.HIGHEST, preferred_element_type=F32,
        ).astype(BF)

    loop(3, lambda k: y_copy(k).wait_send())
    loop(4, lambda k: loop(3, lambda n: x_copy(k, n).wait_send()))

    def ring_sent(k):
        relay_up(k).wait_send()
        to_up(k).wait_send()
        to_down(k).wait_send()

    loop(4, ring_sent)
    loop(3, lambda k: home(k + 1).wait_send())
    loop(8, spread_sent)
    loop(16, column_sent)
    hidden_swap.wait_send()
    m_settle()
    o_settle()
    loop(NC, lambda i: pair_copy(i).wait_send())

    def mate_sent(i):
        mate_copy(c, 0, i).wait_send()
        mate_copy(c, 1, i).wait_send()

    loop(NC, mate_sent)


def shards(tokens, route_token, route_expert, route_gate, w_in, w_out, swap_pairs):
    rows = route_token.shape[0]
    vmem = pl.BlockSpec(memory_space=pltpu.VMEM)
    hbm = pl.BlockSpec(memory_space=pl.ANY)
    dma = pltpu.SemaphoreType.DMA
    mixed, saved = pl.pallas_call(
        kernel,
        out_shape=(
            jax.ShapeDtypeStruct((128, D), BF),
            jax.ShapeDtypeStruct((32, CAP, HS), BF),
        ),
        in_specs=[vmem, vmem, vmem, vmem, vmem, pl.BlockSpec(memory_space=pltpu.SMEM), hbm, hbm],
        out_specs=(vmem, vmem),
        scratch_shapes=[
            pltpu.VMEM((4, CAP, D), BF),
            pltpu.VMEM((4, 4, CAP, D), BF),
            pltpu.VMEM((4, 4, CAP, D), BF),
            pltpu.VMEM((2, 4, 2, 2, CAP, HS), BF),
            pltpu.VMEM((2, 4, 2, 2, CAP, HS), BF),
            pltpu.VMEM((2, 4, 2, 2, CAP, HS), BF),
            pltpu.VMEM((16, 2, CAP, HS), BF),
            pltpu.VMEM((4, CAP, D), BF),
            pltpu.VMEM((4, CAP, D), BF),
            pltpu.VMEM((4, CAP, D), BF),
            pltpu.VMEM((4, CAP, D), BF),
            pltpu.VMEM((4, CAP, D), BF),
            pltpu.VMEM((32, CAP, HS), BF),
            pltpu.VMEM((2, 2, NC, 128, 256), BF),
            pltpu.VMEM((NC, 128, 256), BF),
            pltpu.VMEM((128, 4 * CAP), F32),
            dma((3,)), dma((3,)), dma((4, 3)), dma((4, 3)), dma((4,)), dma((4,)), dma((4,)), dma((4,)), dma((4,)), dma((4,)), dma((4,)), dma((4,)),
            dma((8,)), dma((8,)), dma((16,)), dma((16,)), dma((1,)), dma((1,)),
            dma((NC,)), dma((NC,)), dma((NC,)), dma((NC,)), dma((NC,)), dma((NC,)), dma((NC,)), dma((NC,)),
            dma((2, NC)), dma((2, NC)), dma((NC,)),
            dma((4,)),
        ],
        compiler_params=pltpu.CompilerParams(
            collective_id=0, has_side_effects=True, vmem_limit_bytes=60 * 1024 * 1024
        ),
    )(
        tokens,
        route_token.reshape(1, rows),
        route_expert.reshape(1, rows),
        route_expert,
        route_gate.reshape(1, rows),
        swap_pairs,
        w_in[0],
        w_out[0],
    )
    return mixed, saved.reshape(1, 32 * CAP, HS)


def solution(mesh):
    return jax.shard_map(
        shards,
        mesh=mesh,
        in_specs=(
            P(("rep", "ep"), None),
            P(("rep", "ep")),
            P(("rep", "ep"), None),
            P(("rep", "ep")),
            P("ep", None, None),
            P("ep", None, None),
            P(),
        ),
        out_specs=(P(("rep", "ep"), None), P(("rep", "ep"), None, None)),
        check_vma=False,
    )
```

```python
import jax
import jax.numpy as jnp
from jax import lax
from jax.experimental import pallas as pl
from jax.experimental.pallas import tpu as pltpu
from jax.sharding import PartitionSpec as P

MESH = pl.DeviceIdType.MESH
BF = jnp.bfloat16
F32 = jnp.float32
CAP = 24
D = 3584
HS = 128
DH = D // 2
NI = 14
NO = 7
NC = NI + NO
LAG = 2


def loop(n, body):
    def step(i, carry):
        body(i)
        return carry

    lax.fori_loop(0, n, step, 0)


def kernel(
    tokens, tok_row, exp_row, exp_col, gate_row, swap, w_in, w_out,
    mixed, saved,
    xs, rx, pb, hs, hp, hq, hz, rl, fa, fb, sb, out, ha, wt, tr, gmat,
    ry_send, ry_recv, rx_send, rx_recv, l_send, l_recv, a_send, a_recv, b_send, b_recv, s_send, s_recv, g_send, g_recv, h_send, h_recv, hp_send, hp_recv,
    m_up, m_down, m_recv, o_up, o_down, o_recv, y_send, y_recv, c_send, c_recv, seed, loc,
):
    rep = lax.axis_index("rep")
    ep = lax.axis_index("ep")
    c = lax.rem(rep, 2)
    y = lax.rem(rep // 2, 4)
    xl = rep // 8
    xh = lax.rem(ep, 2)
    z = ep // 2
    x = 2 * xh + xl

    def dev(dx, dy, dz, dc):
        return ((lax.rem(dx, 2) * 4 + dy) * 2 + dc, dz * 2 + dx // 2)

    def swapped(v):
        return v // 2 + 2 * lax.rem(v, 2)

    expert = swapped(y)
    half = lax.rem(y, 2)
    mate = dev(x, y, z, 1 - c)
    pair = dev(x, y + 1 - 2 * half, z, c)
    above = dev(x, y, lax.rem(z + 1, 16), c)
    below = dev(x, y, lax.rem(z + 15, 16), c)
    m_at = lax.rem(z - (4 * expert + 2 * xl + c) + 32, 16)
    o_at = lax.rem(m_at + 8, 16)

    barrier = pltpu.get_barrier_semaphore()

    def greet(target):
        pl.semaphore_signal(barrier, inc=1, device_id=target, device_id_type=MESH)

    def beside(i):
        return i // 4, lax.rem(y + i, 4)

    def greet_column(i):
        @pl.when(i != z)
        def _():
            greet(dev(x, y, i, c))

    def greet_beside(i):
        lo, py = beside(i)

        @pl.when((lo != xl) | (py != y))
        def _():
            greet(dev(2 * xh + lo, py, z, c))

    loop(16, greet_column)
    loop(8, greet_beside)
    loop(3, lambda i: greet(dev(lax.rem(x + i + 1, 4), y, z, c)))
    greet(above)
    greet(below)
    greet(mate)

    own_half = wt.at[c, half]

    def seed_copy(i, dst, act):
        @pl.when(i < NI)
        def _():
            rows_at = pl.ds(pl.multiple_of(DH * half + 128 * i, 128), 128)
            act(pltpu.make_async_copy(w_in.at[rows_at], dst.at[i], seed.at[i]))

        @pl.when(i >= NI)
        def _():
            cols_at = pl.ds(pl.multiple_of(256 * (2 * (i - NI) + half), 256), 256)
            act(pltpu.make_async_copy(w_out.at[:, cols_at], dst.at[i], seed.at[i]))

    for at, dst in ((m_at, own_half), (o_at, tr)):
        @pl.when(at == 0)
        def _():
            loop(NC, lambda i: seed_copy(i, dst, lambda d: d.start()))

    rows = exp_row.shape[1]
    earlier = (exp_col[...] == exp_row[...]) & (
        lax.broadcasted_iota(jnp.int32, (rows, rows), 0)
        < lax.broadcasted_iota(jnp.int32, (rows, rows), 1)
    )
    slot = jnp.sum(earlier.astype(F32), axis=0, keepdims=True).astype(jnp.int32)
    line = lax.shift_right_logical(exp_row[...], 1) + 2 * (exp_row[...] & 1)
    key = line * CAP + slot
    tok_hot = (lax.broadcasted_iota(jnp.int32, (128, rows), 0) == tok_row[...]).astype(F32)
    contract = (((1,), (1,)), ((), ()))
    place_all = (lax.broadcasted_iota(jnp.int32, (4 * CAP, rows), 0) == key).astype(F32)
    gates = lax.dot_general(
        tok_hot * gate_row[...], place_all, contract,
        precision=lax.Precision.HIGHEST, preferred_element_type=F32,
    )
    for n in range(3):
        gmat[n] = gates.astype(BF)
        gates = gates - gmat[n].astype(F32)
    for e in range(4):
        place = (lax.broadcasted_iota(jnp.int32, (CAP, rows), 0) + CAP * e == key).astype(BF)
        pick = lax.dot_general(place, tok_hot.astype(BF), contract, preferred_element_type=F32).astype(BF)
        for n in range(7):
            cols = pl.ds(n * 512, 512)
            xs[e, :, cols] = jnp.dot(pick, tokens[:, cols], preferred_element_type=F32).astype(BF)

    pl.semaphore_wait(barrier, 28)

    def remote(src, dst, send, recv, target):
        return pltpu.make_async_remote_copy(
            src_ref=src, dst_ref=dst, send_sem=send, recv_sem=recv,
            device_id=target, device_id_type=MESH,
        )

    def y_copy(k):
        py = lax.rem(y + k + 1, 4)
        return remote(xs.at[py], rx.at[x, y], ry_send.at[k], ry_recv.at[k], dev(x, py, z, c))

    def x_copy(k, n):
        sy = lax.rem(y + 4 - k, 4)
        return remote(
            rx.at[x, sy], rx.at[x, sy], rx_send.at[k, n], rx_recv.at[k, n],
            dev(lax.rem(x + n + 1, 4), y, z, c),
        )

    def x_arrival(k, n):
        sx, sy = lax.rem(x + 3 - n, 4), lax.rem(y + 4 - k, 4)
        remote(rx.at[sx, sy], rx.at[sx, sy], rx_send.at[k, n], rx_recv.at[k, n], pair).wait_recv()

    loop(3, lambda k: y_copy(k).start())
    mine = pltpu.make_async_copy(xs.at[y], rx.at[x, y], loc.at[2])
    mine.start()

    def stream(buf, at, up, down, recv):
        far = jnp.where(at > 8, 16 - at, at)
        goes_up = at <= 7
        goes_down = (at == 0) | (at >= 10)

        def to_above(i):
            return remote(buf.at[i], buf.at[i], up.at[i], recv.at[i], above)

        def to_below(i):
            return remote(buf.at[i], buf.at[i], down.at[i], recv.at[i], below)

        def pass_on(i):
            @pl.when(at != 0)
            def _():
                to_above(i).wait_recv()

            @pl.when(at == 0)
            def _():
                seed_copy(i, buf, lambda d: d.wait())

            @pl.when(goes_up)
            def _():
                to_above(i).start()

            @pl.when(goes_down)
            def _():
                to_below(i).start()

        def settle():
            @pl.when(goes_up)
            def _():
                loop(NC, lambda i: to_above(i).wait_send())

            @pl.when(goes_down)
            def _():
                loop(NC, lambda i: to_below(i).wait_send())

        return far, pass_on, settle

    m_far, m_pass, m_settle = stream(own_half, m_at, m_up, m_down, m_recv)
    o_far, o_pass, o_settle = stream(tr, o_at, o_up, o_down, o_recv)

    def pair_copy(i):
        return remote(tr.at[i], wt.at[c, half, i], y_send.at[i], y_recv.at[i], pair)

    def pair_arrival(i):
        remote(tr.at[i], wt.at[c, 1 - half, i], y_send.at[i], y_recv.at[i], pair).wait_recv()

    def mate_copy(core, h, j):
        part = wt.at[core, h, pl.ds(NO * j, NO)]
        return remote(part, part, c_send.at[h, j], c_recv.at[h, j], mate)

    def to_mate(h, i):
        @pl.when(lax.rem(i, NO) == NO - 1)
        def _():
            mate_copy(c, h, i // NO).start()

    def when_chunk(i, body):
        @pl.when((i >= 0) & (i < NC))
        def _():
            body(i)

    def mate_arrival(i):
        mate_copy(1 - c, 0, i).wait_recv()
        mate_copy(1 - c, 1, i).wait_recv()

    def activate(sx):
        block = rx[sx].reshape(4 * CAP, D)
        for s in range(2):
            gate_up = jnp.dot(block[:, :DH], wt[s, 0, 0:NI].reshape(DH, 2 * HS), preferred_element_type=F32)
            gate_up += jnp.dot(block[:, DH:], wt[s, 1, 0:NI].reshape(DH, 2 * HS), preferred_element_type=F32)
            v, u = gate_up[:, :HS], gate_up[:, HS:]
            act = (v / (1.0 + jnp.exp(-v)) * u).astype(BF).reshape(4, CAP, HS)
            for sy in range(4):
                hs[lax.rem(sx, 2), sy, s, sx // 2] = act[sy]

    ready_at = jnp.maximum(LAG * m_far + NI + 6, 32)
    hidden_swap = remote(hs, hp, hp_send.at[0], hp_recv.at[0], pair)

    first_slice = 4 * expert + 2 * xl

    def spread_copy(i):
        lo, sy = beside(i)
        src, dst = hq.at[lo, sy], hz.at[pl.ds(first_slice, 2)]
        return (lo == xl) & (sy == y), src, dst, dev(2 * xh + lo, sy, z, c)

    def spread_hidden(i):
        same, src, dst, target = spread_copy(i)

        @pl.when(same)
        def _():
            pltpu.make_async_copy(src, dst, g_recv.at[first_slice // 2]).start()

        @pl.when(jnp.logical_not(same))
        def _():
            remote(src, dst, g_send.at[i], g_recv.at[first_slice // 2], target).start()

    def spread_sent(i):
        same, src, dst, target = spread_copy(i)

        @pl.when(jnp.logical_not(same))
        def _():
            remote(src, dst, g_send.at[i], g_recv.at[first_slice // 2], target).wait_send()

    kept = pl.ds(2 * z, 2)

    def column_copy(i):
        return remote(hz.at[i], ha.at[kept], h_send.at[i], h_recv.at[z], dev(x, y, i, c))

    def send_column(i):
        @pl.when(i == z)
        def _():
            pltpu.make_async_copy(hz.at[i], ha.at[kept], h_recv.at[z]).start()

        @pl.when(i != z)
        def _():
            column_copy(i).start()

    def column_sent(i):
        @pl.when(i != z)
        def _():
            column_copy(i).wait_send()

    def forward_hidden():
        def both(n):
            piece = hz.at[pl.ds(2 * n, 2)]
            pltpu.make_async_copy(piece, piece, g_recv.at[n]).wait()
            send_column(2 * n)
            send_column(2 * n + 1)

        loop(8, both)

    def match_hidden():
        hidden_swap.wait_recv()
        for s in range(2):
            flag = swap[lax.rem(2 * (first_slice + s) + xh, 16)]
            hq[:, :, s] = jnp.where(flag == 1, hp[:, :, s], hs[:, :, s])
        loop(8, spread_hidden)

    match_at = jnp.maximum(LAG * jnp.maximum(m_far, o_far) + NI + 6, 32) + 3

    def tick(t):
        def on_m(i):
            m_pass(i)
            to_mate(half, i)

        def on_o(i):
            o_pass(i)
            pair_copy(i).start()

        def on_y(i):
            pair_arrival(i)
            to_mate(1 - half, i)

        when_chunk(t - LAG * m_far, on_m)
        when_chunk(t - LAG * o_far, on_o)
        when_chunk(t - LAG * m_far - 3, on_y)

        @pl.when(t == ready_at)
        def _():
            loop(NI // NO, mate_arrival)
            loop(4, lambda k: loop(3, lambda n: x_arrival(k, n)))
            loop(4, activate)
            hidden_swap.start()

        @pl.when(t == match_at)
        def _():
            match_hidden()

        @pl.when(t == 0)
        def _():
            mine.wait()
            loop(3, lambda n: x_copy(0, n).start())

        @pl.when(t == jnp.where((m_at == 0) | (o_at == 0), NC + 1, 10))
        def _():
            def second(k):
                sy = lax.rem(y + 3 - k, 4)
                remote(xs.at[sy], rx.at[x, sy], ry_send.at[k], ry_recv.at[k], pair).wait_recv()
                loop(3, lambda n: x_copy(k + 1, n).start())

            loop(3, second)

    loop(NC + 8 * LAG + 3, tick)

    mate_arrival(NI // NO)

    ring_up = dev(lax.rem(x + 1, 4), y, z, c)
    ring_down = dev(lax.rem(x + 3, 4), y, z, c)
    far_x, up_x, down_x = lax.rem(x + 2, 4), lax.rem(x + 1, 4), lax.rem(x + 3, 4)

    def row_of(k):
        return lax.rem(y + k, 4)

    def partials(sx):
        parts = [
            jnp.concatenate([hs[lax.rem(sx, 2), sy, s, sx // 2] for sy in range(4)], axis=0)
            for s in range(2)
        ]
        for n in range(14):
            partial = jnp.dot(parts[0], wt[0, n % 2, NI + n // 2], preferred_element_type=F32)
            partial += jnp.dot(parts[1], wt[1, n % 2, NI + n // 2], preferred_element_type=F32)
            pb[sx, :, :, pl.ds(n * 256, 256)] = partial.astype(BF).reshape(4, CAP, 256)

    def relay_up(k):
        return remote(pb.at[far_x, row_of(k)], rl.at[k], l_send.at[k], l_recv.at[k], ring_up)

    def relay_down(k):
        return remote(pb.at[far_x, row_of(k)], rl.at[k], l_send.at[k], l_recv.at[k], ring_down)

    def to_up(k):
        return remote(pb.at[up_x, row_of(k)], fa.at[k], a_send.at[k], a_recv.at[k], ring_up)

    def to_down(k):
        return remote(pb.at[down_x, row_of(k)], fb.at[k], b_send.at[k], b_recv.at[k], ring_down)

    def home(k):
        return remote(sb.at[k], out.at[y], s_send.at[k], s_recv.at[k], dev(x, row_of(k), z, c))

    def stage(g):
        partials(lax.rem(x + g, 4))

        @pl.when(g == 2)
        def _():
            relay_down(2).start()
            relay_up(1).start()
            relay_down(3).start()
            relay_up(0).start()

        @pl.when(g == 1)
        def _():
            to_up(2).start()
            to_up(3).start()

        @pl.when(g == 3)
        def _():
            to_down(1).start()
            to_down(0).start()
            forward_hidden()

    loop(4, lambda i: stage(jnp.where(i == 0, 2, jnp.where(i == 1, 1, jnp.where(i == 2, 3, 0)))))

    loop(3, lambda k: y_copy(k).wait_send())
    loop(4, lambda k: loop(3, lambda n: x_copy(k, n).wait_send()))
    m_settle()
    o_settle()
    loop(NC, lambda i: pair_copy(i).wait_send())

    def mate_sent(i):
        mate_copy(c, 0, i).wait_send()
        mate_copy(c, 1, i).wait_send()

    loop(NC // NO, mate_sent)

    def add_up(k):
        relay_up(k).wait_recv()
        row = row_of(k)
        pb[up_x, row] = (pb[up_x, row].astype(F32) + rl[k].astype(F32)).astype(BF)
        to_up(k).start()

    def add_down(k):
        relay_down(k).wait_recv()
        row = row_of(k)
        pb[down_x, row] = (pb[down_x, row].astype(F32) + rl[k].astype(F32)).astype(BF)
        to_down(k).start()

    def adds(i):
        add_down(2 + i)
        add_up(1 - i)

    loop(2, adds)

    def finish(i):
        k = jnp.where(i == 0, 2, jnp.where(i == 1, 1, jnp.where(i == 2, 3, 0)))
        to_up(k).wait_recv()
        to_down(k).wait_recv()
        total = pb[x, row_of(k)].astype(F32) + fa[k].astype(F32) + fb[k].astype(F32)

        @pl.when(k > 0)
        def _():
            sb[k] = total.astype(BF)
            home(k).start()

        @pl.when(k == 0)
        def _():
            out[y] = total.astype(BF)

    loop(4, finish)

    def hidden_arrival(q):
        pair_of = pl.ds(2 * q, 2)
        pltpu.make_async_copy(ha.at[pair_of], ha.at[pair_of], h_recv.at[q]).wait()

    loop(16, hidden_arrival)
    saved[...] = ha[...]

    def home_arrival(k):
        remote(sb.at[k], out.at[lax.rem(y + 4 - k, 4)], s_send.at[k], s_recv.at[k], pair).wait_recv()

    loop(3, lambda k: home_arrival(k + 1))
    for n in range(7):
        cols = pl.ds(n * 512, 512)
        rows_out = out[:, :, cols].astype(F32).reshape(4 * CAP, 512).astype(BF)
        mixed[:, cols] = sum(
            jnp.dot(gmat[m], rows_out, preferred_element_type=F32) for m in (2, 1, 0)
        ).astype(BF)


    def ring_sent(k):
        relay_up(k).wait_send()
        to_up(k).wait_send()
        to_down(k).wait_send()

    loop(4, ring_sent)
    loop(3, lambda k: home(k + 1).wait_send())
    loop(8, spread_sent)
    loop(16, column_sent)
    hidden_swap.wait_send()


def shards(tokens, route_token, route_expert, route_gate, w_in, w_out, swap_pairs):
    rows = route_token.shape[0]
    vmem = pl.BlockSpec(memory_space=pltpu.VMEM)
    hbm = pl.BlockSpec(memory_space=pl.ANY)
    dma = pltpu.SemaphoreType.DMA
    mixed, saved = pl.pallas_call(
        kernel,
        out_shape=(
            jax.ShapeDtypeStruct((128, D), BF),
            jax.ShapeDtypeStruct((32, CAP, HS), BF),
        ),
        in_specs=[vmem, vmem, vmem, vmem, vmem, pl.BlockSpec(memory_space=pltpu.SMEM), hbm, hbm],
        out_specs=(vmem, vmem),
        scratch_shapes=[
            pltpu.VMEM((4, CAP, D), BF),
            pltpu.VMEM((4, 4, CAP, D), BF),
            pltpu.VMEM((4, 4, CAP, D), BF),
            pltpu.VMEM((2, 4, 2, 2, CAP, HS), BF),
            pltpu.VMEM((2, 4, 2, 2, CAP, HS), BF),
            pltpu.VMEM((2, 4, 2, 2, CAP, HS), BF),
            pltpu.VMEM((16, 2, CAP, HS), BF),
            pltpu.VMEM((4, CAP, D), BF),
            pltpu.VMEM((4, CAP, D), BF),
            pltpu.VMEM((4, CAP, D), BF),
            pltpu.VMEM((4, CAP, D), BF),
            pltpu.VMEM((4, CAP, D), BF),
            pltpu.VMEM((32, CAP, HS), BF),
            pltpu.VMEM((2, 2, NC, 128, 256), BF),
            pltpu.VMEM((NC, 128, 256), BF),
            pltpu.VMEM((3, 128, 4 * CAP), BF),
            dma((3,)), dma((3,)), dma((4, 3)), dma((4, 3)), dma((4,)), dma((4,)), dma((4,)), dma((4,)), dma((4,)), dma((4,)), dma((4,)), dma((4,)),
            dma((8,)), dma((8,)), dma((16,)), dma((16,)), dma((1,)), dma((1,)),
            dma((NC,)), dma((NC,)), dma((NC,)), dma((NC,)), dma((NC,)), dma((NC,)), dma((NC,)), dma((NC,)),
            dma((2, NC // NO)), dma((2, NC // NO)), dma((NC,)),
            dma((4,)),
        ],
        compiler_params=pltpu.CompilerParams(
            collective_id=0, has_side_effects=True, vmem_limit_bytes=60 * 1024 * 1024
        ),
    )(
        tokens,
        route_token.reshape(1, rows),
        route_expert.reshape(1, rows),
        route_expert,
        route_gate.reshape(1, rows),
        swap_pairs,
        w_in[0],
        w_out[0],
    )
    return mixed, saved.reshape(1, 32 * CAP, HS)


def solution(mesh):
    return jax.shard_map(
        shards,
        mesh=mesh,
        in_specs=(
            P(("rep", "ep"), None),
            P(("rep", "ep")),
            P(("rep", "ep"), None),
            P(("rep", "ep")),
            P("ep", None, None),
            P("ep", None, None),
            P(),
        ),
        out_specs=(P(("rep", "ep"), None), P(("rep", "ep"), None, None)),
        check_vma=False,
    )
```

```python
import jax
import jax.numpy as jnp
from jax import lax
from jax.experimental import pallas as pl
from jax.experimental.pallas import tpu as pltpu
from jax.sharding import PartitionSpec as P

MESH = pl.DeviceIdType.MESH
BF = jnp.bfloat16
F32 = jnp.float32
CAP = 24
D = 3584
HS = 128
DH = D // 2
NI = 14
NO = 7
NC = NI + NO
LAG = 2


def loop(n, body):
    def step(i, carry):
        body(i)
        return carry

    lax.fori_loop(0, n, step, 0)


def kernel(
    tokens, tok_row, exp_row, gate_row, swap, w_in, w_out,
    mixed, saved,
    xs, rx, pb, hs, hp, hq, hz, rl, fa, fb, sb, out, ha, wt, tr, gmat,
    ry_send, ry_recv, rx_send, rx_recv, l_send, l_recv, a_send, a_recv, b_send, b_recv, s_send, s_recv, g_send, g_recv, h_send, h_recv, hp_send, hp_recv,
    m_up, m_down, m_recv, o_up, o_down, o_recv, y_send, y_recv, c_send, c_recv, seed, loc,
):
    rep = lax.axis_index("rep")
    ep = lax.axis_index("ep")
    c = lax.rem(rep, 2)
    y = lax.rem(rep // 2, 4)
    xl = rep // 8
    xh = lax.rem(ep, 2)
    z = ep // 2
    x = 2 * xh + xl

    def dev(dx, dy, dz, dc):
        return ((lax.rem(dx, 2) * 4 + dy) * 2 + dc, dz * 2 + dx // 2)

    def swapped(v):
        return v // 2 + 2 * lax.rem(v, 2)

    expert = swapped(y)
    half = lax.rem(y, 2)
    mate = dev(x, y, z, 1 - c)
    pair = dev(x, y + 1 - 2 * half, z, c)
    above = dev(x, y, lax.rem(z + 1, 16), c)
    below = dev(x, y, lax.rem(z + 15, 16), c)
    m_at = lax.rem(z - (4 * expert + 2 * xl + c) + 32, 16)
    o_at = lax.rem(m_at + 8, 16)

    barrier = pltpu.get_barrier_semaphore()

    def greet(target):
        pl.semaphore_signal(barrier, inc=1, device_id=target, device_id_type=MESH)

    def beside(i):
        return i // 4, lax.rem(y + i, 4)

    def greet_column(i):
        @pl.when(i != z)
        def _():
            greet(dev(x, y, i, c))

    def greet_beside(i):
        lo, py = beside(i)

        @pl.when((lo != xl) | (py != y))
        def _():
            greet(dev(2 * xh + lo, py, z, c))

    loop(16, greet_column)
    loop(8, greet_beside)
    loop(3, lambda i: greet(dev(lax.rem(x + i + 1, 4), y, z, c)))
    greet(above)
    greet(below)
    greet(mate)

    own_half = wt.at[c, half]

    def seed_copy(i, dst, act):
        @pl.when(i < NI)
        def _():
            rows_at = pl.ds(pl.multiple_of(DH * half + 128 * i, 128), 128)
            act(pltpu.make_async_copy(w_in.at[rows_at], dst.at[i], seed.at[i]))

        @pl.when(i >= NI)
        def _():
            cols_at = pl.ds(pl.multiple_of(256 * (2 * (i - NI) + half), 256), 256)
            act(pltpu.make_async_copy(w_out.at[:, cols_at], dst.at[i], seed.at[i]))

    for at, dst in ((m_at, own_half), (o_at, tr)):
        @pl.when(at == 0)
        def _():
            loop(NC, lambda i: seed_copy(i, dst, lambda d: d.start()))

    rows = exp_row.shape[1]
    earlier = (
        lax.broadcasted_iota(jnp.int32, (rows, rows), 0)
        < lax.broadcasted_iota(jnp.int32, (rows, rows), 1)
    ).astype(F32)
    hits = (lax.broadcasted_iota(jnp.int32, (8, rows), 0) == exp_row[...]).astype(F32)
    counts = jnp.dot(hits, earlier, preferred_element_type=F32)
    slot = jnp.sum(hits * counts, axis=0, keepdims=True).astype(jnp.int32)
    line = lax.shift_right_logical(exp_row[...], 1) + 2 * (exp_row[...] & 1)
    key = line * CAP + slot
    tok_hot = (lax.broadcasted_iota(jnp.int32, (128, rows), 0) == tok_row[...]).astype(F32)
    contract = (((1,), (1,)), ((), ()))
    place_all = (lax.broadcasted_iota(jnp.int32, (4 * CAP, rows), 0) == key).astype(F32)
    gates = lax.dot_general(
        tok_hot * gate_row[...], place_all, contract,
        precision=lax.Precision.HIGHEST, preferred_element_type=F32,
    )
    for n in range(3):
        gmat[n] = gates.astype(BF)
        gates = gates - gmat[n].astype(F32)
    for e in range(4):
        place = (lax.broadcasted_iota(jnp.int32, (CAP, rows), 0) + CAP * e == key).astype(BF)
        pick = lax.dot_general(place, tok_hot.astype(BF), contract, preferred_element_type=F32).astype(BF)
        for n in range(7):
            cols = pl.ds(n * 512, 512)
            xs[e, :, cols] = jnp.dot(pick, tokens[:, cols], preferred_element_type=F32).astype(BF)

    pl.semaphore_wait(barrier, 28)

    def remote(src, dst, send, recv, target):
        return pltpu.make_async_remote_copy(
            src_ref=src, dst_ref=dst, send_sem=send, recv_sem=recv,
            device_id=target, device_id_type=MESH,
        )

    def y_copy(k):
        py = lax.rem(y + k + 1, 4)
        return remote(xs.at[py], rx.at[x, y], ry_send.at[k], ry_recv.at[k], dev(x, py, z, c))

    def x_copy(k, n):
        sy = lax.rem(y + 4 - k, 4)
        return remote(
            rx.at[x, sy], rx.at[x, sy], rx_send.at[k, n], rx_recv.at[k, n],
            dev(lax.rem(x + n + 1, 4), y, z, c),
        )

    def x_arrival(k, n):
        sx, sy = lax.rem(x + 3 - n, 4), lax.rem(y + 4 - k, 4)
        remote(rx.at[sx, sy], rx.at[sx, sy], rx_send.at[k, n], rx_recv.at[k, n], pair).wait_recv()

    loop(3, lambda k: y_copy(k).start())
    mine = pltpu.make_async_copy(xs.at[y], rx.at[x, y], loc.at[2])
    mine.start()

    def stream(buf, at, up, down, recv):
        far = jnp.where(at > 8, 16 - at, at)
        goes_up = at <= 7
        goes_down = (at == 0) | (at >= 10)

        def to_above(i):
            return remote(buf.at[i], buf.at[i], up.at[i], recv.at[i], above)

        def to_below(i):
            return remote(buf.at[i], buf.at[i], down.at[i], recv.at[i], below)

        def pass_on(i):
            @pl.when(at != 0)
            def _():
                to_above(i).wait_recv()

            @pl.when(at == 0)
            def _():
                seed_copy(i, buf, lambda d: d.wait())

            @pl.when(goes_up)
            def _():
                to_above(i).start()

            @pl.when(goes_down)
            def _():
                to_below(i).start()

        def settle():
            @pl.when(goes_up)
            def _():
                loop(NC, lambda i: to_above(i).wait_send())

            @pl.when(goes_down)
            def _():
                loop(NC, lambda i: to_below(i).wait_send())

        return far, pass_on, settle

    m_far, m_pass, m_settle = stream(own_half, m_at, m_up, m_down, m_recv)
    o_far, o_pass, o_settle = stream(tr, o_at, o_up, o_down, o_recv)

    def pair_copy(i):
        return remote(tr.at[i], wt.at[c, half, i], y_send.at[i], y_recv.at[i], pair)

    def pair_arrival(i):
        remote(tr.at[i], wt.at[c, 1 - half, i], y_send.at[i], y_recv.at[i], pair).wait_recv()

    def mate_copy(core, h, j):
        part = wt.at[core, h, pl.ds(NO * j, NO)]
        return remote(part, part, c_send.at[h, j], c_recv.at[h, j], mate)

    def to_mate(h, i):
        @pl.when(lax.rem(i, NO) == NO - 1)
        def _():
            mate_copy(c, h, i // NO).start()

    def when_chunk(i, body):
        @pl.when((i >= 0) & (i < NC))
        def _():
            body(i)

    def mate_arrival(i):
        mate_copy(1 - c, 0, i).wait_recv()
        mate_copy(1 - c, 1, i).wait_recv()

    def activate(sx):
        block = rx[sx].reshape(4 * CAP, D)
        for s in range(2):
            gate_up = jnp.dot(block[:, :DH], wt[s, 0, 0:NI].reshape(DH, 2 * HS), preferred_element_type=F32)
            gate_up += jnp.dot(block[:, DH:], wt[s, 1, 0:NI].reshape(DH, 2 * HS), preferred_element_type=F32)
            v, u = gate_up[:, :HS], gate_up[:, HS:]
            act = (v / (1.0 + jnp.exp(-v)) * u).astype(BF).reshape(4, CAP, HS)
            for sy in range(4):
                hs[lax.rem(sx, 2), sy, s, sx // 2] = act[sy]

    ready_at = jnp.maximum(LAG * m_far + NI + 6, 32)
    hidden_swap = remote(hs, hp, hp_send.at[0], hp_recv.at[0], pair)

    first_slice = 4 * expert + 2 * xl

    def spread_copy(i):
        lo, sy = beside(i)
        src, dst = hq.at[lo, sy], hz.at[pl.ds(first_slice, 2)]
        return (lo == xl) & (sy == y), src, dst, dev(2 * xh + lo, sy, z, c)

    def spread_hidden(i):
        same, src, dst, target = spread_copy(i)

        @pl.when(same)
        def _():
            pltpu.make_async_copy(src, dst, g_recv.at[first_slice // 2]).start()

        @pl.when(jnp.logical_not(same))
        def _():
            remote(src, dst, g_send.at[i], g_recv.at[first_slice // 2], target).start()

    def spread_sent(i):
        same, src, dst, target = spread_copy(i)

        @pl.when(jnp.logical_not(same))
        def _():
            remote(src, dst, g_send.at[i], g_recv.at[first_slice // 2], target).wait_send()

    kept = pl.ds(2 * z, 2)

    def column_copy(i):
        return remote(hz.at[i], ha.at[kept], h_send.at[i], h_recv.at[z], dev(x, y, i, c))

    def send_column(i):
        @pl.when(i == z)
        def _():
            pltpu.make_async_copy(hz.at[i], ha.at[kept], h_recv.at[z]).start()

        @pl.when(i != z)
        def _():
            column_copy(i).start()

    def column_sent(i):
        @pl.when(i != z)
        def _():
            column_copy(i).wait_send()

    def forward_hidden():
        def both(n):
            piece = hz.at[pl.ds(2 * n, 2)]
            pltpu.make_async_copy(piece, piece, g_recv.at[n]).wait()
            send_column(2 * n)
            send_column(2 * n + 1)

        loop(8, both)

    def match_hidden():
        hidden_swap.wait_recv()
        for s in range(2):
            flag = swap[lax.rem(2 * (first_slice + s) + xh, 16)]
            hq[:, :, s] = jnp.where(flag == 1, hp[:, :, s], hs[:, :, s])
        loop(8, spread_hidden)

    match_at = jnp.maximum(LAG * jnp.maximum(m_far, o_far) + NI + 6, 32) + 3

    def tick(t):
        def on_m(i):
            m_pass(i)
            to_mate(half, i)

        def on_o(i):
            o_pass(i)
            pair_copy(i).start()

        def on_y(i):
            pair_arrival(i)
            to_mate(1 - half, i)

        when_chunk(t - LAG * m_far, on_m)
        when_chunk(t - LAG * o_far, on_o)
        when_chunk(t - LAG * m_far - 3, on_y)

        @pl.when(t == ready_at)
        def _():
            loop(NI // NO, mate_arrival)
            loop(4, lambda k: loop(3, lambda n: x_arrival(k, n)))
            loop(4, activate)
            hidden_swap.start()

        @pl.when(t == match_at)
        def _():
            match_hidden()

        @pl.when(t == 0)
        def _():
            mine.wait()
            loop(3, lambda n: x_copy(0, n).start())

        @pl.when(t == jnp.where((m_at == 0) | (o_at == 0), NC + 1, 10))
        def _():
            def second(k):
                sy = lax.rem(y + 3 - k, 4)
                remote(xs.at[sy], rx.at[x, sy], ry_send.at[k], ry_recv.at[k], pair).wait_recv()
                loop(3, lambda n: x_copy(k + 1, n).start())

            loop(3, second)

    loop(NC + 8 * LAG + 3, tick)

    mate_arrival(NI // NO)

    ring_up = dev(lax.rem(x + 1, 4), y, z, c)
    ring_down = dev(lax.rem(x + 3, 4), y, z, c)
    far_x, up_x, down_x = lax.rem(x + 2, 4), lax.rem(x + 1, 4), lax.rem(x + 3, 4)

    def row_of(k):
        return lax.rem(y + k, 4)

    def partials(sx):
        parts = [
            jnp.concatenate([hs[lax.rem(sx, 2), sy, s, sx // 2] for sy in range(4)], axis=0)
            for s in range(2)
        ]
        for n in range(14):
            partial = jnp.dot(parts[0], wt[0, n % 2, NI + n // 2], preferred_element_type=F32)
            partial += jnp.dot(parts[1], wt[1, n % 2, NI + n // 2], preferred_element_type=F32)
            pb[sx, :, :, pl.ds(n * 256, 256)] = partial.astype(BF).reshape(4, CAP, 256)

    def relay_up(k):
        return remote(pb.at[far_x, row_of(k)], rl.at[k], l_send.at[k], l_recv.at[k], ring_up)

    def relay_down(k):
        return remote(pb.at[far_x, row_of(k)], rl.at[k], l_send.at[k], l_recv.at[k], ring_down)

    def to_up(k):
        return remote(pb.at[up_x, row_of(k)], fa.at[k], a_send.at[k], a_recv.at[k], ring_up)

    def to_down(k):
        return remote(pb.at[down_x, row_of(k)], fb.at[k], b_send.at[k], b_recv.at[k], ring_down)

    def home(k):
        return remote(sb.at[k], out.at[y], s_send.at[k], s_recv.at[k], dev(x, row_of(k), z, c))

    def stage(g):
        partials(lax.rem(x + g, 4))

        @pl.when(g == 2)
        def _():
            relay_down(2).start()
            relay_up(1).start()
            relay_down(3).start()
            relay_up(0).start()

        @pl.when(g == 1)
        def _():
            to_up(2).start()
            to_up(3).start()

        @pl.when(g == 3)
        def _():
            to_down(1).start()
            to_down(0).start()
            forward_hidden()

    loop(4, lambda i: stage(jnp.where(i == 0, 2, jnp.where(i == 1, 1, jnp.where(i == 2, 3, 0)))))

    loop(3, lambda k: y_copy(k).wait_send())
    loop(4, lambda k: loop(3, lambda n: x_copy(k, n).wait_send()))
    m_settle()
    o_settle()
    loop(NC, lambda i: pair_copy(i).wait_send())

    def mate_sent(i):
        mate_copy(c, 0, i).wait_send()
        mate_copy(c, 1, i).wait_send()

    loop(NC // NO, mate_sent)

    def add_up(k):
        relay_up(k).wait_recv()
        row = row_of(k)
        pb[up_x, row] = (pb[up_x, row].astype(F32) + rl[k].astype(F32)).astype(BF)
        to_up(k).start()

    def add_down(k):
        relay_down(k).wait_recv()
        row = row_of(k)
        pb[down_x, row] = (pb[down_x, row].astype(F32) + rl[k].astype(F32)).astype(BF)
        to_down(k).start()

    def adds(i):
        add_down(2 + i)
        add_up(1 - i)

    loop(2, adds)

    def finish(i):
        k = jnp.where(i == 0, 2, jnp.where(i == 1, 1, jnp.where(i == 2, 3, 0)))
        to_up(k).wait_recv()
        to_down(k).wait_recv()
        total = pb[x, row_of(k)].astype(F32) + fa[k].astype(F32) + fb[k].astype(F32)

        @pl.when(k > 0)
        def _():
            sb[k] = total.astype(BF)
            home(k).start()

        @pl.when(k == 0)
        def _():
            out[y] = total.astype(BF)

    loop(4, finish)

    def hidden_arrival(q):
        pair_of = pl.ds(2 * q, 2)
        pltpu.make_async_copy(ha.at[pair_of], ha.at[pair_of], h_recv.at[q]).wait()

    loop(16, hidden_arrival)
    saved[...] = ha[...]

    def home_arrival(k):
        remote(sb.at[k], out.at[lax.rem(y + 4 - k, 4)], s_send.at[k], s_recv.at[k], pair).wait_recv()

    loop(3, lambda k: home_arrival(k + 1))
    for n in range(7):
        cols = pl.ds(n * 512, 512)
        rows_out = out[:, :, cols].astype(F32).reshape(4 * CAP, 512).astype(BF)
        mixed[:, cols] = sum(
            jnp.dot(gmat[m], rows_out, preferred_element_type=F32) for m in (2, 1, 0)
        ).astype(BF)


    def ring_sent(k):
        relay_up(k).wait_send()
        to_up(k).wait_send()
        to_down(k).wait_send()

    loop(4, ring_sent)
    loop(3, lambda k: home(k + 1).wait_send())
    loop(8, spread_sent)
    loop(16, column_sent)
    hidden_swap.wait_send()


def shards(tokens, route_token, route_expert, route_gate, w_in, w_out, swap_pairs):
    rows = route_token.shape[0]
    vmem = pl.BlockSpec(memory_space=pltpu.VMEM)
    hbm = pl.BlockSpec(memory_space=pl.ANY)
    dma = pltpu.SemaphoreType.DMA
    mixed, saved = pl.pallas_call(
        kernel,
        out_shape=(
            jax.ShapeDtypeStruct((128, D), BF),
            jax.ShapeDtypeStruct((32, CAP, HS), BF),
        ),
        in_specs=[vmem, vmem, vmem, vmem, pl.BlockSpec(memory_space=pltpu.SMEM), hbm, hbm],
        out_specs=(vmem, vmem),
        scratch_shapes=[
            pltpu.VMEM((4, CAP, D), BF),
            pltpu.VMEM((4, 4, CAP, D), BF),
            pltpu.VMEM((4, 4, CAP, D), BF),
            pltpu.VMEM((2, 4, 2, 2, CAP, HS), BF),
            pltpu.VMEM((2, 4, 2, 2, CAP, HS), BF),
            pltpu.VMEM((2, 4, 2, 2, CAP, HS), BF),
            pltpu.VMEM((16, 2, CAP, HS), BF),
            pltpu.VMEM((4, CAP, D), BF),
            pltpu.VMEM((4, CAP, D), BF),
            pltpu.VMEM((4, CAP, D), BF),
            pltpu.VMEM((4, CAP, D), BF),
            pltpu.VMEM((4, CAP, D), BF),
            pltpu.VMEM((32, CAP, HS), BF),
            pltpu.VMEM((2, 2, NC, 128, 256), BF),
            pltpu.VMEM((NC, 128, 256), BF),
            pltpu.VMEM((3, 128, 4 * CAP), BF),
            dma((3,)), dma((3,)), dma((4, 3)), dma((4, 3)), dma((4,)), dma((4,)), dma((4,)), dma((4,)), dma((4,)), dma((4,)), dma((4,)), dma((4,)),
            dma((8,)), dma((8,)), dma((16,)), dma((16,)), dma((1,)), dma((1,)),
            dma((NC,)), dma((NC,)), dma((NC,)), dma((NC,)), dma((NC,)), dma((NC,)), dma((NC,)), dma((NC,)),
            dma((2, NC // NO)), dma((2, NC // NO)), dma((NC,)),
            dma((4,)),
        ],
        compiler_params=pltpu.CompilerParams(
            collective_id=0, has_side_effects=True, vmem_limit_bytes=60 * 1024 * 1024
        ),
    )(
        tokens,
        route_token.reshape(1, rows),
        route_expert.reshape(1, rows),
        route_gate.reshape(1, rows),
        swap_pairs,
        w_in[0],
        w_out[0],
    )
    return mixed, saved.reshape(1, 32 * CAP, HS)


def solution(mesh):
    return jax.shard_map(
        shards,
        mesh=mesh,
        in_specs=(
            P(("rep", "ep"), None),
            P(("rep", "ep")),
            P(("rep", "ep"), None),
            P(("rep", "ep")),
            P("ep", None, None),
            P("ep", None, None),
            P(),
        ),
        out_specs=(P(("rep", "ep"), None), P(("rep", "ep"), None, None)),
        check_vma=False,
    )
```
